128 devices in a mesh: lat: 8 (over y, core), lon: 16 (over z, x).
Axes of the slice: x: 4, y: 4, z: 4, core: 2. Of those that a mesh axis runs over, the one named last changes fastest.
Arguments:
- covariates: bfloat16 [12, 512, 8192], P(None, 'lat', 'lon'), may hold values from -6 to 6
- w_in: bfloat16 [12, 64], replicated, may hold values from -1.75 to 1.75
- b_in: float32 [64], replicated, may hold values from -3 to 3
- w_out: float32 [64], replicated, may hold values from -2 to 2
- b_out: float32 [1], replicated, may hold values from -1 to 1
- unit_ids: int32 [512, 8192], P('lat', 'lon'), may hold values from 0 to 1023, as said below
- unit_counts: int32 [1024], P(('lat', 'lon')), may hold values from 64 to 1023
Outputs:
- density: float32 [512, 8192], P('lat', 'lon')
The draws below stay inside these ranges and needn't reach their ends.
Inputs may be any that keep to these rules, and one draw needn't show every extreme that they name: `unit_ids`: the grid is cut into blocks of 64 x 64 cells aligned at multiples of 64; each block belongs to exactly one unit and each unit to exactly one block, the pairing drawn from the seed. Every cell of unit u lies within 2 rows and 2 columns of u's block, and every unit owns at least one cell.
All inputs are finite; a program needn't handle non-finite values.
Results may differ from the reference program's by a relative error of at most 0.0003.
Values sent between devices are 32-bit elements; how exact they have to be, the bound alone decides.
A program may use at most 64 MiB of HBM per device.

```python
import math
import jax
import jax.numpy as jnp
from jax import lax

COV = 12
HID = 64
BLK = 64
ROUNDS = 3
NLAT = 512
NLON = 8192
UNITS = 1024


def draw_unit_ids(key, part):
    key_rows, key_cols, key_perm = jax.random.split(key, 3)
    rows = jnp.arange(NLAT, dtype=jnp.int32)[:, None] + jax.random.randint(key_rows, (NLAT, NLON), -2, 3, dtype=jnp.int32)
    cols = jnp.arange(NLON, dtype=jnp.int32)[None, :] + jax.random.randint(key_cols, (NLAT, NLON), -2, 3, dtype=jnp.int32)
    rows = jnp.clip(rows, 0, NLAT - 1) // BLK
    cols = jnp.clip(cols, 0, NLON - 1) // BLK
    block = rows * (NLON // BLK) + cols
    order = jax.random.permutation(key_perm, UNITS).astype(jnp.int32)
    return order[block].astype(jnp.int32)


def plant(entries, key, low, top_value):
    extent = entries.shape
    place = [jax.random.randint(jax.random.fold_in(key, axis), (), 0, extent[axis]) for axis in range(len(extent))]
    entries = entries.at[tuple(place)].set(low)
    longest = extent.index(max(extent))
    place[longest] = (place[longest] + 1) % extent[longest]
    return entries.at[tuple(place)].set(top_value)


def block_levels(stream_key, dims, cuts, least, top_value):
    loudness, own = 1.0, jax.random.fold_in(stream_key, 6)
    for dim, shards_of in cuts:
        draws = jnp.exp(jax.random.uniform(jax.random.fold_in(own, dim), (shards_of,), jnp.float32, least / len(cuts), top_value / len(cuts)))
        loudness = loudness * jnp.repeat(draws, dims[dim] // shards_of).reshape([-1 if axis == dim else 1 for axis in range(len(dims))])
    return loudness


def bell_draw(key, extent, width, bound, shards=(), kind=jnp.bfloat16):
    entries = width * jax.random.normal(key, extent, jnp.float32)
    if shards:
        entries = entries * block_levels(key, extent, shards, -0.22, 0.18)
    return jnp.clip(entries, -bound, bound).astype(kind)


def setup_inputs(seed: int = 0) -> dict:
    splits = jax.random.split(jax.random.key(seed), 8)
    return {
        "covariates": bell_draw(splits[0], (COV, NLAT, NLON), 1.0, 6.0, ((1, 8), (2, 16))),
        "w_in": bell_draw(splits[1], (COV, HID), COV ** -0.5, 1.75),
        "b_in": bell_draw(splits[2], (HID,), 0.5, 3.0, (), jnp.float32),
        "w_out": bell_draw(splits[3], (HID,), 0.3, 2.0, (), jnp.float32),
        "b_out": jnp.clip(jax.random.uniform(splits[4], (1,), jnp.float32, -1.0, 1.0), -1.0, 1.0),
        "unit_ids": draw_unit_ids(jax.random.fold_in(splits[7], 71), 0),
        "unit_counts": plant(jax.random.randint(splits[6], (UNITS,), 64, 1024), jax.random.fold_in(splits[6], 1), 64, 1023).astype(jnp.int32),
    }


def cell_weight(block, w_in, b_in, w_out, b_out):
    hidden = jnp.einsum('ch,crx->hrx', w_in.astype(jnp.float32), block.astype(jnp.float32), precision=lax.Precision.HIGHEST)
    hidden = jax.nn.silu(hidden + b_in[:, None, None])
    score = jnp.einsum('h,hrx->rx', w_out, hidden, precision=lax.Precision.HIGHEST) + b_out[0]
    return jax.nn.softplus(score)


def box_smooth(field):
    padded = jnp.pad(field, 2)
    rows_n = field.shape[0]
    cols_n = field.shape[1]
    across = padded[0:rows_n + 4, 0:cols_n]
    for shift in range(1, 5):
        across = across + padded[0:rows_n + 4, shift:shift + cols_n]
    total = across[0:rows_n]
    for shift in range(1, 5):
        total = total + across[shift:shift + rows_n]
    return total / 25.0


def reference(covariates, w_in, b_in, w_out, b_out, unit_ids, unit_counts):
    nrows = covariates.shape[1]
    ncols = covariates.shape[2]
    step_rows = math.gcd(nrows, 64)

    def one_block(index):
        block = lax.dynamic_slice_in_dim(covariates, index * step_rows, step_rows, 1)
        return cell_weight(block, w_in, b_in, w_out, b_out)

    weight = lax.map(one_block, jnp.arange(nrows // step_rows, dtype=jnp.int32)).reshape(nrows, ncols)
    units_n = unit_counts.shape[0]
    counts_f = unit_counts.astype(jnp.float32)
    flat_ids = unit_ids.reshape(-1)

    def renorm(field):
        totals = jax.ops.segment_sum(field.reshape(-1), flat_ids, num_segments=units_n)
        factor = counts_f / totals
        return field * factor[unit_ids]

    field = renorm(weight)
    for round_index in range(ROUNDS):
        field = renorm(box_smooth(field))
    return field
```

```python
import functools

import jax
import jax.numpy as jnp
from jax import lax
from jax.experimental import pallas as pl
from jax.experimental.pallas import tpu as pltpu
from jax.sharding import PartitionSpec as P

BLK = 64
ROUNDS = 3
M = 8
GR = 16
HC = 16
MESH = pl.DeviceIdType.MESH
DIRS = ((-1, 0), (1, 0), (0, 1), (0, -1), (-1, 1), (-1, -1), (1, 1), (1, -1))


def opposite(k):
    return DIRS.index((-DIRS[k][0], -DIRS[k][1]))


def halo_copies(buf, east, west, send, recv, peer, rows, cols):
    top, bot = slice(M, 2 * M), slice(rows, rows + M)
    far = slice(rows + M, rows + 2 * M)
    near = slice(0, M)
    mid = slice(M, rows + M)
    first, last = slice(0, 128), slice(cols - 128, cols)
    full = slice(0, cols)
    moves = (
        (buf.at[top, full], buf.at[far, full]),
        (buf.at[bot, full], buf.at[near, full]),
        (buf.at[mid, last], west.at[mid]),
        (buf.at[mid, first], east.at[mid]),
        (buf.at[top, last], west.at[far]),
        (buf.at[top, first], east.at[far]),
        (buf.at[bot, last], west.at[near]),
        (buf.at[bot, first], east.at[near]),
    )
    return [
        pltpu.make_async_remote_copy(
            src_ref=src,
            dst_ref=dst,
            send_sem=send.at[k],
            recv_sem=recv.at[k],
            device_id=peer(*DIRS[k]),
            device_id_type=MESH,
        )
        for k, (src, dst) in enumerate(moves)
    ]


def lane_rows(mids, east0, west7):
    lane = lax.broadcasted_iota(jnp.int32, (1, 128), 1)
    half = lane < 64
    left = (lane % 64) < 32
    tiles = len(mids) // 2
    ext = [west7] + list(mids) + [east0]
    own, alt = [], []
    for t in range(tiles):
        own.append(jnp.where(half, ext[2 * t + 1], ext[2 * t + 2]))
        low = jnp.where(left, ext[2 * t], ext[2 * t + 2])
        high = jnp.where(left, ext[2 * t + 1], ext[2 * t + 3])
        alt.append(jnp.where(half, low, high))
    own.append(jnp.where(half, east0, west7))
    alt.append(jnp.where(half, mids[-1], mids[0]))
    return jnp.concatenate(own, axis=1), jnp.concatenate(alt, axis=1)


def kernel(
    lat_n, lon_n, cov_hbm, win_ref, bin_ref, wout_ref, bout_ref, ids_hbm, cnt_ref, out_ref,
    xbuf, lbuf, ids, iwest, ieast, idx, wbuf, wwest, weast, sbuf, cown, crow, cslot_a, cslot_b,
    fsend, frecv, xsem, isem, isend, irecv, wsend, wrecv, asend, arecv, bsend, brecv, fs, fr,
):
    cov_n, rows, cols = cov_hbm.shape
    hid = win_ref.shape[1]
    kdim = cov_n * GR
    groups = rows // GR
    ext_rows, ext_cols = rows + 2 * M, cols + 128
    units = cols // BLK
    lat = lax.axis_index("lat")
    lon = lax.axis_index("lon")

    def peer(dlat, dlon):
        return (lax.rem(lat + (dlat + lat_n), lat_n), lax.rem(lon + (dlon + lon_n), lon_n))

    xcopies = []
    for g in range(groups):
        band = pl.ds(g * GR, GR)
        xcopies.append(
            pltpu.make_async_copy(cov_hbm.at[:, band], xbuf.at[:, band], xsem.at[g])
        )
    icopy = pltpu.make_async_copy(ids_hbm, ids.at[M : M + rows, 0:cols], isem)
    icopy.start()
    for copy in xcopies:
        copy.start()

    barrier = pltpu.get_barrier_semaphore()
    greet = [(d, 0) for d in range(1, lat_n)] + [(0, d) for d in range(1, lon_n)]
    greet += [(-1, -1), (-1, 1), (1, -1), (1, 1)]
    for move in greet:
        pl.semaphore_signal(barrier, inc=1, device_id=peer(*move), device_id_type=MESH)

    sub = lax.broadcasted_iota(jnp.int32, (8, 128), 0)
    lane = lax.broadcasted_iota(jnp.int32, (8, 128), 1)
    mine = jnp.zeros((8, 128), jnp.float32)
    for k in range(units):
        mine = jnp.where(lane == lon * units + k, cnt_ref[k].astype(jnp.float32), mine)
    cown[...] = jnp.where(sub == lat, mine, 0.0)

    bias = bin_ref[...] * 0.5
    b0 = bias.astype(jnp.bfloat16).astype(jnp.float32)
    b1 = (bias - b0).astype(jnp.bfloat16).astype(jnp.float32)
    b2 = bias - b0 - b1
    params = jnp.concatenate(
        [win_ref[...].astype(jnp.float32) * 0.5, b0, b1, b2, jnp.zeros_like(b0)], axis=0
    )
    kx = kdim + GR
    src = lax.broadcasted_iota(jnp.int32, (16, kx), 0)
    dst = lax.broadcasted_iota(jnp.int32, (16, kx), 1)
    pick = jnp.where(dst < kdim, dst // GR, dst - kdim + cov_n) == src
    spread = lax.dot_general(
        params.astype(jnp.bfloat16),
        pick.astype(jnp.bfloat16),
        (((0,), (0,)), ((), ())),
        preferred_element_type=jnp.float32,
    )
    drow = lax.broadcasted_iota(jnp.int32, (GR, kx), 0)
    dcol = lax.broadcasted_iota(jnp.int32, (GR, kx), 1)
    diag = (dcol >= kdim) | (dcol % GR == drow)
    for h in range(hid):
        row = jnp.broadcast_to(spread[h : h + 1, :], (GR, kx))
        lbuf[h * GR : (h + 1) * GR, :] = jnp.where(diag, row, 0.0).astype(jnp.bfloat16)

    icopy.wait()
    pl.semaphore_wait(barrier, len(greet))
    icopies = halo_copies(ids, ieast, iwest, isend, irecv, peer, rows, cols)
    acopies = [
        pltpu.make_async_remote_copy(
            src_ref=cown, dst_ref=cslot_a.at[d - 1], send_sem=asend.at[d - 1],
            recv_sem=arecv.at[d - 1], device_id=peer(d, 0), device_id_type=MESH,
        )
        for d in range(1, lat_n)
    ]
    for copy in acopies + icopies:
        copy.start()

    ones = jnp.ones((GR, cols), jnp.bfloat16)

    def network(g):
        xcopies[g].wait()
        x = xbuf[:, g * GR : (g + 1) * GR, :].reshape(kdim, cols)
        x = jnp.concatenate([x, ones], axis=0)

        def chunk(i, acc):
            left = lbuf[pl.ds(pl.multiple_of(i * HC * GR, HC * GR), HC * GR), :]
            v = jnp.dot(left, x, preferred_element_type=jnp.float32)
            for h in range(HC):
                u = v[h * GR : (h + 1) * GR, :]
                acc = acc + (u + u * jnp.tanh(u)) * wout_ref[i * HC + h]
            return acc

        score = lax.fori_loop(0, hid // HC, chunk, jnp.zeros((GR, cols), jnp.float32))
        score = score + bout_ref[0]
        y = jnp.exp(-jnp.abs(score))
        z = y / (2.0 + y)
        q = z * z
        poly = jnp.float32(1.0 / 15)
        for n in (13, 11, 9, 7, 5, 3, 1):
            poly = poly * q + jnp.float32(1.0 / n)
        wbuf[M + g * GR : M + (g + 1) * GR, 0:cols] = jnp.maximum(score, 0.0) + 2.0 * z * poly

    order = [0, groups - 1] + list(range(1, groups - 1))
    bcopies = []
    for step, g in enumerate(order):
        network(g)
        if step == 1:
            for copy in acopies:
                copy.wait_recv()
            total = cown[...]
            for d in range(1, lat_n):
                total = total + cslot_a[d - 1]
            crow[...] = total
            bcopies = [
                pltpu.make_async_remote_copy(
                    src_ref=crow, dst_ref=cslot_b.at[d - 1], send_sem=bsend.at[d - 1],
                    recv_sem=brecv.at[d - 1], device_id=peer(0, d), device_id_type=MESH,
                )
                for d in range(1, lon_n)
            ]
            for copy in bcopies:
                copy.start()

    wcopies = halo_copies(wbuf, weast, wwest, wsend, wrecv, peer, rows, cols)
    for copy in wcopies:
        copy.start()

    for copy in icopies:
        copy.wait_recv()
    lane_x = lax.broadcasted_iota(jnp.int32, (ext_rows, 128), 1)
    row_x = lax.broadcasted_iota(jnp.int32, (ext_rows, ext_cols), 0)
    wrap = jnp.where(lane_x < 64, ieast[...], iwest[...])
    keep_e = (lane_x < M) & (lon < lon_n - 1)
    keep_w = (lane_x >= 128 - M) & (lon > 0)
    wrap = jnp.where(keep_e | keep_w, wrap, -1)
    whole = jnp.concatenate([ids[:, 0:cols], wrap], axis=1)
    gone = ((row_x < M) & (lat == 0)) | ((row_x >= M + rows) & (lat == lat_n - 1))
    idx[...] = jnp.where(gone, -1, whole)

    picks = (M // 2 - 1, M + BLK // 2, M + rows + M // 2)
    id_rows = []
    homes = None
    for r in picks:
        mids = []
        for j in range(units):
            c = j * BLK + BLK // 2
            mids.append(ids[r : r + 1, c // 128 * 128 : c // 128 * 128 + 128][:, c % 128 : c % 128 + 1])
        if r == picks[1]:
            homes = mids
        e0 = ieast[r : r + 1, :][:, 32:33]
        w7 = iwest[r : r + 1, :][:, 96:97]
        id_rows.append(lane_rows(mids, e0, w7))

    for copy in bcopies:
        copy.wait_recv()
    table = crow[...]
    for d in range(1, lon_n):
        table = table + cslot_b[d - 1]
    uid = jnp.where(lane < units * lon_n, sub * (units * lon_n) + lane, -1)
    found = jnp.zeros((8, 128), jnp.float32)
    for j in range(units):
        hit = jnp.sum(jnp.where(uid == homes[j], table, 0.0), axis=0, keepdims=True)
        found = jnp.where(sub == j, hit, found)
    counts = jnp.sum(found, axis=1, keepdims=True)

    (ion, ian), (iom, iam), (ios, ias) = id_rows
    right_half = (lax.broadcasted_iota(jnp.int32, (8, ext_cols), 1) % 64) >= 32
    own_half = [(sub // 2 == t) & ((sub % 2 == 1) == (lane >= 64)) for t in range(cols // 128)]

    def factors(field, r):
        cell_ids = idx[...]
        part = jnp.where(cell_ids == iom, field, 0.0).reshape(ext_rows // 8, 8, ext_cols)
        side = jnp.where(cell_ids == iam, field, 0.0).reshape(ext_rows // 8, 8, ext_cols)
        part = jnp.sum(part, axis=0)
        side = jnp.sum(side, axis=0)
        part = part + pltpu.roll(jnp.where(right_half, side, 0.0), 2, 1)
        part = part + pltpu.roll(jnp.where(right_half, 0.0, side), ext_cols - 2, 1)
        rowsum = jnp.sum(part, axis=0, keepdims=True)
        gathered = jnp.zeros((8, 128), jnp.float32)
        for t in range(cols // 128):
            gathered = jnp.where(own_half[t], rowsum[:, t * 128 : t * 128 + 128], gathered)
        totals = jnp.sum(gathered, axis=1, keepdims=True)
        fsend[r] = jnp.broadcast_to(counts / totals, (8, 128))
        copies = [
            pltpu.make_async_remote_copy(
                src_ref=fsend.at[r], dst_ref=frecv.at[r, opposite(k)], send_sem=fs.at[r, k],
                recv_sem=fr.at[r, opposite(k)], device_id=peer(*DIRS[k]), device_id_type=MESH,
            )
            for k in range(8)
        ]
        for copy in copies:
            copy.start()
        return copies

    def spread_rows(r, row_dirs):
        center, east, west = row_dirs
        mids = []
        for j in range(units):
            if center is None:
                mids.append(fsend[r, j : j + 1, :])
            else:
                mids.append(frecv[r, center, j : j + 1, :])
        return lane_rows(mids, frecv[r, east, 0:1, :], frecv[r, west, units - 1 : units, :])

    def scaled(field, r):
        fon, fan = spread_rows(r, (0, 4, 5))
        fom, fam = spread_rows(r, (None, 2, 3))
        fos, fas = spread_rows(r, (1, 6, 7))
        cell_ids = idx[...]
        fac = jnp.where(cell_ids == iam, fam, 0.0)
        fac = jnp.where(cell_ids == iom, fom, fac)
        band = 2 * M
        head, tail = fac[0:band], fac[ext_rows - band :]
        hid_ids, tid_ids = cell_ids[0:band], cell_ids[ext_rows - band :]
        head = jnp.where(hid_ids == ian, fan, head)
        head = jnp.where(hid_ids == ion, fon, head)
        tail = jnp.where(tid_ids == ias, fas, tail)
        tail = jnp.where(tid_ids == ios, fos, tail)
        fac = jnp.concatenate([head, fac[band : ext_rows - band], tail], axis=0)
        return field * fac

    def smooth(field):
        pair = field + pltpu.roll(field, 1, 0)
        down = field + pltpu.roll(pair, 1, 0) + pltpu.roll(pair, ext_rows - 2, 0)
        pair = down + pltpu.roll(down, 1, 1)
        both = down + pltpu.roll(pair, 1, 1) + pltpu.roll(pair, ext_cols - 2, 1)
        return both * jnp.float32(1.0 / 25.0)

    for copy in wcopies:
        copy.wait_recv()
    wrap = jnp.where(lane_x < 64, weast[...], wwest[...])
    sbuf[...] = jnp.concatenate([wbuf[:, 0:cols], wrap], axis=1)

    pending = []
    for r in range(ROUNDS + 1):
        copies = factors(sbuf[...], r)
        for copy in copies:
            copy.wait_recv()
        pending += copies
        if r < ROUNDS:
            sbuf[...] = smooth(scaled(sbuf[...], r))
    out_ref[...] = scaled(sbuf[...], ROUNDS)[M : M + rows, 0:cols]

    for copy in icopies + acopies + bcopies + wcopies + pending:
        copy.wait_send()


def shards(covariates, w_in, b_in, w_out, b_out, unit_ids, unit_counts):
    lat_n = lax.axis_size("lat")
    lon_n = lax.axis_size("lon")
    cov_n, rows, cols = covariates.shape
    hid = w_in.shape[1]
    ext_rows, ext_cols = rows + 2 * M, cols + 128
    kx = cov_n * GR + GR
    f32, i32 = jnp.float32, jnp.int32
    vmem = pl.BlockSpec(memory_space=pltpu.VMEM)
    smem = pl.BlockSpec(memory_space=pltpu.SMEM)
    hbm = pl.BlockSpec(memory_space=pl.ANY)
    dma = pltpu.SemaphoreType.DMA
    return pl.pallas_call(
        functools.partial(kernel, lat_n, lon_n),
        out_shape=jax.ShapeDtypeStruct((rows, cols), f32),
        in_specs=[hbm, vmem, vmem, smem, smem, hbm, smem],
        out_specs=vmem,
        scratch_shapes=[
            pltpu.VMEM((cov_n, rows, cols), jnp.bfloat16),
            pltpu.VMEM((hid * GR, kx), jnp.bfloat16),
            pltpu.VMEM((ext_rows, ext_cols), i32),
            pltpu.VMEM((ext_rows, 128), i32),
            pltpu.VMEM((ext_rows, 128), i32),
            pltpu.VMEM((ext_rows, ext_cols), i32),
            pltpu.VMEM((ext_rows, ext_cols), f32),
            pltpu.VMEM((ext_rows, 128), f32),
            pltpu.VMEM((ext_rows, 128), f32),
            pltpu.VMEM((ext_rows, ext_cols), f32),
            pltpu.VMEM((8, 128), f32),
            pltpu.VMEM((8, 128), f32),
            pltpu.VMEM((lat_n - 1, 8, 128), f32),
            pltpu.VMEM((lon_n - 1, 8, 128), f32),
            pltpu.VMEM((ROUNDS + 1, 8, 128), f32),
            pltpu.VMEM((ROUNDS + 1, 8, 8, 128), f32),
            dma((rows // GR,)),
            dma(()),
            dma((8,)),
            dma((8,)),
            dma((8,)),
            dma((8,)),
            dma((lat_n - 1,)),
            dma((lat_n - 1,)),
            dma((lon_n - 1,)),
            dma((lon_n - 1,)),
            dma((ROUNDS + 1, 8)),
            dma((ROUNDS + 1, 8)),
        ],
        compiler_params=pltpu.CompilerParams(
            collective_id=0, has_side_effects=True, vmem_limit_bytes=40 * 1024 * 1024
        ),
    )(covariates, w_in, b_in.reshape(1, hid), w_out, b_out, unit_ids, unit_counts)


def solution(mesh):
    return jax.shard_map(
        shards,
        mesh=mesh,
        in_specs=(P(None, "lat", "lon"), P(), P(), P(), P(), P("lat", "lon"), P(("lat", "lon"))),
        out_specs=P("lat", "lon"),
        check_vma=False,
    )
```

```python
import functools

import jax
import jax.numpy as jnp
from jax import lax
from jax.experimental import pallas as pl
from jax.experimental.pallas import tpu as pltpu
from jax.sharding import PartitionSpec as P

BLK = 64
ROUNDS = 3
M = 8
GR = 16
MESH = pl.DeviceIdType.MESH
DIRS = ((-1, 0), (1, 0), (0, 1), (0, -1), (-1, 1), (-1, -1), (1, 1), (1, -1))


FAR = tuple((a, b) for b in (-1, 1, 0) for a in (-2, 2, -1, 1, 0) if (a, b) != (0, 0))


def halo_copies(buf, east, west, send, recv, peer, rows, cols):
    top, bot = slice(M, 2 * M), slice(rows, rows + M)
    far = slice(rows + M, rows + 2 * M)
    near = slice(0, M)
    mid = slice(M, rows + M)
    first, last = slice(0, 128), slice(cols - 128, cols)
    full = slice(0, cols)
    moves = (
        (buf.at[top, full], buf.at[far, full]),
        (buf.at[bot, full], buf.at[near, full]),
        (buf.at[mid, last], west.at[mid]),
        (buf.at[mid, first], east.at[mid]),
        (buf.at[top, last], west.at[far]),
        (buf.at[top, first], east.at[far]),
        (buf.at[bot, last], west.at[near]),
        (buf.at[bot, first], east.at[near]),
    )
    return [
        pltpu.make_async_remote_copy(
            src_ref=src,
            dst_ref=dst,
            send_sem=send.at[k],
            recv_sem=recv.at[k],
            device_id=peer(*DIRS[k]),
            device_id_type=MESH,
        )
        for k, (src, dst) in enumerate(moves)
    ]


def lane_rows(units):
    lane = lax.broadcasted_iota(jnp.int32, (1, 128), 1)
    n = len(units)
    even = [jnp.where(lane < 96, units[t], units[(t + 2) % n]) for t in range(0, n, 2)]
    odd = [jnp.where(lane < 32, units[t - 1], units[t + 1]) for t in range(0, n, 2)]
    return jnp.concatenate(even, axis=1), jnp.concatenate(odd, axis=1)


def kernel(
    lat_n, lon_n, cov_hbm, win_hbm, bin_hbm, wout_hbm, bout_hbm, ids_hbm, cnt_hbm, out_ref,
    xbuf, win_ref, bin_ref, wout_ref, bout_ref, cnt_ref, lbuf, ids, iwest, ieast, code,
    wbuf, wwest, weast, sbuf, reach, homes, cown, crow, cslot_a, cslot_b, cbuf, ebuf, fbuf,
    xsem, psem, isem, isend, irecv, hsend, hrecv, wsend, wrecv, asend, arecv, bsend, brecv,
    esend, erecv,
):
    cov_n, rows, cols = cov_hbm.shape
    hid = win_ref.shape[1]
    kdim = cov_n * GR
    groups = rows // GR
    ext_rows, ext_cols = rows + 2 * M, cols + 128
    units = cols // BLK
    tiles = cols // 128
    lat = lax.axis_index("lat")
    lon = lax.axis_index("lon")

    def peer(dlat, dlon):
        return (lax.rem(lat + (dlat + lat_n), lat_n), lax.rem(lon + (dlon + lon_n), lon_n))

    barrier = pltpu.get_barrier_semaphore()
    greet = [(d, 0) for d in range(1, lat_n)] + [(0, d) for d in range(1, lon_n)]
    greet += [(a, b) for a, b in FAR if a != 0 and b != 0]
    for move in greet:
        pl.semaphore_signal(barrier, inc=1, device_id=peer(*move), device_id_type=MESH)

    pcopies = [
        pltpu.make_async_copy(src, dst, psem.at[k])
        for k, (src, dst) in enumerate(
            (
                (win_hbm, win_ref), (bin_hbm, bin_ref), (wout_hbm, wout_ref),
                (bout_hbm, bout_ref), (cnt_hbm, cnt_ref),
            )
        )
    ]
    for copy in pcopies:
        copy.start()
    xcopies = []
    for g in range(groups):
        band = pl.ds(g * GR, GR)
        xcopies.append(
            pltpu.make_async_copy(cov_hbm.at[:, band], xbuf.at[:, band], xsem.at[g])
        )
        xcopies[g].start()
    icopy = pltpu.make_async_copy(ids_hbm, ids.at[M : M + rows, 0:cols], isem)
    icopy.start()
    for copy in pcopies:
        copy.wait()

    sub = lax.broadcasted_iota(jnp.int32, (8, 128), 0)
    lane = lax.broadcasted_iota(jnp.int32, (8, 128), 1)
    mine = jnp.zeros((8, 128), jnp.float32)
    for k in range(units):
        mine = jnp.where(lane == lon * units + k, cnt_ref[k].astype(jnp.float32), mine)
    cown[...] = jnp.where(sub == lat, mine, 0.0)

    bias = bin_ref[...] * 0.5
    b0 = bias.astype(jnp.bfloat16).astype(jnp.float32)
    b1 = (bias - b0).astype(jnp.bfloat16).astype(jnp.float32)
    b2 = bias - b0 - b1
    params = jnp.concatenate(
        [win_ref[...].astype(jnp.float32) * 0.5, b0, b1, b2, jnp.zeros_like(b0)], axis=0
    )
    kx = kdim + GR
    src = lax.broadcasted_iota(jnp.int32, (16, kx), 0)
    dst = lax.broadcasted_iota(jnp.int32, (16, kx), 1)
    pick = jnp.where(dst < kdim, dst // GR, dst - kdim + cov_n) == src
    spread = lax.dot_general(
        params.astype(jnp.bfloat16),
        pick.astype(jnp.bfloat16),
        (((0,), (0,)), ((), ())),
        preferred_element_type=jnp.float32,
    )
    drow = lax.broadcasted_iota(jnp.int32, (GR, kx), 0)
    dcol = lax.broadcasted_iota(jnp.int32, (GR, kx), 1)
    diag = (dcol >= kdim) | (dcol % GR == drow)
    for h in range(hid):
        row = jnp.broadcast_to(spread[h : h + 1, :], (GR, kx))
        lbuf[h * GR : (h + 1) * GR, :] = jnp.where(diag, row, 0.0).astype(jnp.bfloat16)

    ones = jnp.ones((GR, cols), jnp.bfloat16)

    def network(g):
        xcopies[g].wait()
        x = xbuf[:, g * GR : (g + 1) * GR, :].reshape(kdim, cols)
        x = jnp.concatenate([x, ones], axis=0)

        v = jnp.dot(lbuf[...], x, preferred_element_type=jnp.float32)
        score = jnp.zeros((GR, cols), jnp.float32)
        for h in range(hid):
            u = v[h * GR : (h + 1) * GR, :]
            score = score + (u + u * jnp.tanh(u)) * wout_ref[h]
        score = score + bout_ref[0]
        y = jnp.exp(-jnp.abs(score))
        z = y / (2.0 + y)
        q = z * z
        poly = jnp.float32(1.0 / 15)
        for n in (13, 11, 9, 7, 5, 3, 1):
            poly = poly * q + jnp.float32(1.0 / n)
        wbuf[M + g * GR : M + (g + 1) * GR, 0:cols] = jnp.maximum(score, 0.0) + 2.0 * z * poly

    for g in range(groups):
        network(g)

    icopy.wait()
    home = jnp.zeros((8, 128), jnp.int32)
    for j in range(units):
        c = j * BLK + BLK // 2
        at = ids[M + BLK // 2 : M + BLK // 2 + 1, c // 128 * 128 : c // 128 * 128 + 128]
        home = jnp.where(sub == j, at[:, c % 128 : c % 128 + 1], home)
    homes[2, 8:16, :] = home

    def far_copies(buf, send, recv):
        return [
            pltpu.make_async_remote_copy(
                src_ref=buf.at[2, 8:16],
                dst_ref=buf.at[2 - a, 8 * (1 - b) : 8 * (1 - b) + 8],
                send_sem=send.at[k],
                recv_sem=recv.at[k],
                device_id=peer(a, b),
                device_id_type=MESH,
            )
            for k, (a, b) in enumerate(FAR)
        ]

    def row_copies(src, dst, send, recv, moves):
        return [
            pltpu.make_async_remote_copy(
                src_ref=src, dst_ref=dst.at[k], send_sem=send.at[k], recv_sem=recv.at[k],
                device_id=peer(*move), device_id_type=MESH,
            )
            for k, move in enumerate(moves)
        ]

    pl.semaphore_wait(barrier, len(greet))
    acopies = row_copies(cown, cslot_a, asend, arecv, [(d, 0) for d in range(1, lat_n)])
    icopies = halo_copies(ids, ieast, iwest, isend, irecv, peer, rows, cols)
    hcopies = far_copies(homes, hsend, hrecv)
    wcopies = halo_copies(wbuf, weast, wwest, wsend, wrecv, peer, rows, cols)
    for copy in acopies + icopies + hcopies + wcopies:
        copy.start()

    for copy in acopies:
        copy.wait_recv()
    total = cown[...]
    for d in range(1, lat_n):
        total = total + cslot_a[d - 1]
    crow[...] = total
    bcopies = row_copies(crow, cslot_b, bsend, brecv, [(0, d) for d in range(1, lon_n)])
    for copy in bcopies:
        copy.start()

    def ring_rows(buf, r):
        order = list(range(8, 8 + units + 1)) + [7]
        return lane_rows([buf[r, s : s + 1, :] for s in order])

    def smooth(field):
        pair = field + pltpu.roll(field, 1, 0)
        down = field + pltpu.roll(pair, 1, 0) + pltpu.roll(pair, ext_rows - 2, 0)
        pair = down + pltpu.roll(down, 1, 1)
        both = down + pltpu.roll(pair, 1, 1) + pltpu.roll(pair, ext_cols - 2, 1)
        return both * jnp.float32(1.0 / 25.0)

    for copy in icopies + hcopies:
        copy.wait_recv()
    lane_x = lax.broadcasted_iota(jnp.int32, (ext_rows, 128), 1)
    row_x = lax.broadcasted_iota(jnp.int32, (ext_rows, ext_cols), 0)
    wrap = jnp.where(lane_x < 64, ieast[...], iwest[...])
    keep_e = (lane_x < M) & (lon < lon_n - 1)
    keep_w = (lane_x >= 128 - M) & (lon > 0)
    wrap = jnp.where(keep_e | keep_w, wrap, -1)
    whole = jnp.concatenate([ids[:, 0:cols], wrap], axis=1)
    gone = ((row_x < M) & (lat == 0)) | ((row_x >= M + rows) & (lat == lat_n - 1))
    whole = jnp.where(gone, -1, whole)
    band = 2 * M

    def classed(which, picked, base, other):
        even, odd = picked
        return jnp.where(which == even, base, jnp.where(which == odd, base + 1, other))

    kinds = classed(whole, ring_rows(homes, 2), 0, -1)
    code[...] = kinds
    code[0:band] = classed(whole[0:band], ring_rows(homes, 1), 2, kinds[0:band])
    code[ext_rows - band :] = classed(
        whole[ext_rows - band :], ring_rows(homes, 3), 4, kinds[ext_rows - band :]
    )
    for p in range(2):
        reach[p] = smooth(jnp.where(code[...] == p, 1.0, 0.0))

    def fold(x):
        return jnp.sum(x.reshape(x.shape[0] // 8, 8, ext_cols), axis=0)

    def census(field, k):
        kind = code[...]
        sums = [jnp.zeros((8, 128), jnp.float32)] * 7
        for p in range(2):
            near = field * reach[p]
            head, tail = near[0:band], near[ext_rows - band :]
            hkind, tkind = kind[0:band], kind[ext_rows - band :]
            parts = [fold(jnp.where(kind == p, field, 0.0))]
            for v in (p, 1 - p):
                parts.append(fold(jnp.where(hkind == 2 + v, head, 0.0)))
                parts.append(fold(jnp.where(kind == v, near, 0.0)))
                parts.append(fold(jnp.where(tkind == 4 + v, tail, 0.0)))
            for q in range(7):
                turned = pltpu.roll(parts[q], 32 if p == 0 else ext_cols - 32, 1)
                line = jnp.sum(turned, axis=0, keepdims=True)
                for t in range(tiles):
                    sums[q] = jnp.where(
                        sub == 2 * t + p, line[:, t * 128 : t * 128 + 128], sums[q]
                    )
        ebuf[k, 2, 8:16, 0:128] = jnp.broadcast_to(
            jnp.sum(sums[0], axis=1, keepdims=True), (8, 128)
        )
        links = jnp.zeros((8, 128), jnp.float32)
        for d in range(3):
            cross = sums[4 + d]
            for b, x in enumerate(
                (jnp.where(lane < 64, cross, 0.0), sums[1 + d], jnp.where(lane < 64, 0.0, cross))
            ):
                links = jnp.where(lane == 3 * d + b, jnp.sum(x, axis=1, keepdims=True), links)
        ebuf[k, 2, 8:16, 128:256] = links
        copies = far_copies(ebuf.at[k], esend.at[k], erecv.at[k])
        for copy in copies:
            copy.start()
        return copies

    lane_u = lax.broadcasted_iota(jnp.int32, (24, 128), 1)

    def solve(k):
        first = [cbuf[r] / ebuf[k, r, :, 0:128] for r in range(5)]
        for r in range(1, 4):
            fbuf[2 * k, r - 1] = first[r]
            mix = jnp.zeros((24, 128), jnp.float32)
            for a in range(3):
                for b in range(3):
                    f = first[r + a - 1]
                    f = f if b == 1 else pltpu.roll(f, 1 if b == 0 else 23, 0)
                    mix = jnp.where(lane_u == 3 * a + b, f, mix)
            second = jnp.sum(mix * ebuf[k, r, :, 128:256], axis=1, keepdims=True)
            fbuf[2 * k + 1, r - 1] = cbuf[r] / second

    def scaled(field, i):
        kind = code[...]
        rows_f = [ring_rows(fbuf.at[i], r) for r in range(3)]

        def chosen(which, base, picked, other):
            return jnp.where(
                which == base, picked[0], jnp.where(which == base + 1, picked[1], other)
            )

        fac = chosen(kind, 0, rows_f[1], 0.0)
        head = chosen(kind[0:band], 2, rows_f[0], fac[0:band])
        tail = chosen(kind[ext_rows - band :], 4, rows_f[2], fac[ext_rows - band :])
        fac = jnp.concatenate([head, fac[band : ext_rows - band], tail], axis=0)
        return field * fac

    for copy in wcopies:
        copy.wait_recv()
    wrap = jnp.where(lane_x < 64, weast[...], wwest[...])
    sbuf[...] = jnp.concatenate([wbuf[:, 0:cols], wrap], axis=1)
    pending = census(sbuf[...], 0)

    for copy in bcopies:
        copy.wait_recv()
    table = crow[...]
    for d in range(1, lon_n):
        table = table + cslot_b[d - 1]
    uid = jnp.where(lane < units * lon_n, sub * (units * lon_n) + lane, -1)

    def look(r, carry):
        found = [jnp.zeros((8, 128), jnp.float32)] * 3
        for s in range(6, 10 + units):
            hit = jnp.where(uid == homes[r, s : s + 1, :], table, 0.0)
            hit = jnp.sum(hit, axis=0, keepdims=True)
            found[s // 8] = jnp.where(sub == s % 8, hit, found[s // 8])
        for i in range(3):
            cbuf[r, 8 * i : 8 * i + 8, :] = jnp.broadcast_to(
                jnp.sum(found[i], axis=1, keepdims=True), (8, 128)
            )
        return carry

    lax.fori_loop(0, 5, look, 0)

    for k in range((ROUNDS + 1) // 2):
        if k > 0:
            pending = census(sbuf[...], k)
        for copy in pending:
            copy.wait_recv()
        solve(k)
        sbuf[...] = smooth(scaled(sbuf[...], 2 * k))
        if 2 * k + 1 < ROUNDS:
            sbuf[...] = smooth(scaled(sbuf[...], 2 * k + 1))
        if k == 0:
            sent = pending
    out_ref[...] = scaled(sbuf[...], ROUNDS)[M : M + rows, 0:cols]

    for copy in icopies + hcopies + acopies + bcopies + wcopies + sent + pending:
        copy.wait_send()


def shards(covariates, w_in, b_in, w_out, b_out, unit_ids, unit_counts):
    lat_n = lax.axis_size("lat")
    lon_n = lax.axis_size("lon")
    cov_n, rows, cols = covariates.shape
    hid = w_in.shape[1]
    ext_rows, ext_cols = rows + 2 * M, cols + 128
    kx = cov_n * GR + GR
    f32, i32, bf16 = jnp.float32, jnp.int32, jnp.bfloat16
    hbm = pl.BlockSpec(memory_space=pltpu.HBM)
    dma = pltpu.SemaphoreType.DMA
    pairs = (ROUNDS + 1) // 2
    far = len(FAR)
    return pl.pallas_call(
        functools.partial(kernel, lat_n, lon_n),
        out_shape=pltpu.VMEM((rows, cols), f32),
        in_specs=[hbm] * 7,
        out_specs=pl.BlockSpec(memory_space=pltpu.VMEM),
        scratch_shapes=[
            pltpu.VMEM((cov_n, rows, cols), bf16),
            pltpu.VMEM((cov_n, hid), bf16),
            pltpu.VMEM((1, hid), f32),
            pltpu.SMEM((hid,), f32),
            pltpu.SMEM((1,), f32),
            pltpu.SMEM((unit_counts.shape[0],), i32),
            pltpu.VMEM((hid * GR, kx), bf16),
            pltpu.VMEM((ext_rows, ext_cols), i32),
            pltpu.VMEM((ext_rows, 128), i32),
            pltpu.VMEM((ext_rows, 128), i32),
            pltpu.VMEM((ext_rows, ext_cols), i32),
            pltpu.VMEM((ext_rows, ext_cols), f32),
            pltpu.VMEM((ext_rows, 128), f32),
            pltpu.VMEM((ext_rows, 128), f32),
            pltpu.VMEM((ext_rows, ext_cols), f32),
            pltpu.VMEM((2, ext_rows, ext_cols), f32),
            pltpu.VMEM((5, 24, 128), i32),
            pltpu.VMEM((8, 128), f32),
            pltpu.VMEM((8, 128), f32),
            pltpu.VMEM((lat_n - 1, 8, 128), f32),
            pltpu.VMEM((lon_n - 1, 8, 128), f32),
            pltpu.VMEM((5, 24, 128), f32),
            pltpu.VMEM((pairs, 5, 24, 256), f32),
            pltpu.VMEM((2 * pairs, 3, 24, 128), f32),
            dma((rows // GR,)),
            dma((5,)),
            dma(()),
            dma((8,)),
            dma((8,)),
            dma((far,)),
            dma((far,)),
            dma((8,)),
            dma((8,)),
            dma((lat_n - 1,)),
            dma((lat_n - 1,)),
            dma((lon_n - 1,)),
            dma((lon_n - 1,)),
            dma((pairs, far)),
            dma((pairs, far)),
        ],
        compiler_params=pltpu.CompilerParams(
            collective_id=0, has_side_effects=True, vmem_limit_bytes=60 * 1024 * 1024
        ),
    )(covariates, w_in, b_in.reshape(1, hid), w_out, b_out, unit_ids, unit_counts)


def solution(mesh):
    return jax.shard_map(
        shards,
        mesh=mesh,
        in_specs=(P(None, "lat", "lon"), P(), P(), P(), P(), P("lat", "lon"), P(("lat", "lon"))),
        out_specs=P("lat", "lon"),
        check_vma=False,
    )
```

```python
import functools

import jax
import jax.numpy as jnp
from jax import lax
from jax.experimental import pallas as pl
from jax.experimental.pallas import tpu as pltpu
from jax.sharding import PartitionSpec as P

BLK = 64
ROUNDS = 3
M = 8
GR = 16
LIN = 3
MESH = pl.DeviceIdType.MESH
DIRS = ((-1, 1), (-1, -1), (1, 1), (1, -1), (0, 1), (0, -1), (-1, 0), (1, 0))


FAR = tuple((a, b) for b in (-1, 1, 0) for a in (-2, 2, -1, 1, 0) if (a, b) != (0, 0))


def halo_copies(buf, east, west, send, recv, peer, rows, cols):
    top, bot = slice(M, 2 * M), slice(rows, rows + M)
    far = slice(rows + M, rows + 2 * M)
    near = slice(0, M)
    mid = slice(M, rows + M)
    first, last = slice(0, 128), slice(cols - 128, cols)
    full = slice(0, cols)
    every = slice(None)
    moves = (
        (buf.at[every, top, last], west.at[every, far]),
        (buf.at[every, top, first], east.at[every, far]),
        (buf.at[every, bot, last], west.at[every, near]),
        (buf.at[every, bot, first], east.at[every, near]),
        (buf.at[every, mid, last], west.at[every, mid]),
        (buf.at[every, mid, first], east.at[every, mid]),
        (buf.at[every, top, full], buf.at[every, far, full]),
        (buf.at[every, bot, full], buf.at[every, near, full]),
    )
    return [
        pltpu.make_async_remote_copy(
            src_ref=src,
            dst_ref=dst,
            send_sem=send.at[k],
            recv_sem=recv.at[k],
            device_id=peer(*DIRS[k]),
            device_id_type=MESH,
        )
        for k, (src, dst) in enumerate(moves)
    ]


def lane_rows(units):
    lane = lax.broadcasted_iota(jnp.int32, (1, 128), 1)
    n = len(units)
    even = [jnp.where(lane < 96, units[t], units[(t + 2) % n]) for t in range(0, n, 2)]
    odd = [jnp.where(lane < 32, units[t - 1], units[t + 1]) for t in range(0, n, 2)]
    return jnp.concatenate(even, axis=1), jnp.concatenate(odd, axis=1)


def kernel(
    lat_n, lon_n, cov_hbm, win_hbm, bin_hbm, wvec_hbm, wout_hbm, bout_hbm, ids_hbm, cnt_hbm, out_ref,
    xbuf, win_ref, bin_ref, wvec_ref, wout_ref, bout_ref, cnt_ref, lbuf, ids, halo, hwest, heast,
    code, sbuf, reach, homes, cown, crow, cslot_a, cslot_b, cbuf, ebuf, fbuf,
    xsem, psem, isem, hsend, hrecv, asend, arecv, bsend, brecv, esend, erecv,
):
    cov_n, rows, cols = cov_hbm.shape
    hid = win_ref.shape[1]
    kdim = cov_n * GR
    groups = rows // GR
    ext_rows, ext_cols = rows + 2 * M, cols + 128
    units = cols // BLK
    tiles = cols // 128
    lat = lax.axis_index("lat")
    lon = lax.axis_index("lon")

    def peer(dlat, dlon):
        return (lax.rem(lat + (dlat + lat_n), lat_n), lax.rem(lon + (dlon + lon_n), lon_n))

    barrier = pltpu.get_barrier_semaphore()
    greet = [(a, b) for a, b in FAR if a != 0 and b != 0]
    greet += [(0, d) for d in range(1, lon_n)] + [(d, 0) for d in range(1, lat_n)]
    for move in greet:
        pl.semaphore_signal(barrier, inc=1, device_id=peer(*move), device_id_type=MESH)

    pcopies = [
        pltpu.make_async_copy(src, dst, psem.at[k])
        for k, (src, dst) in enumerate(
            (
                (win_hbm, win_ref), (bin_hbm, bin_ref), (wvec_hbm, wvec_ref),
                (wout_hbm, wout_ref), (bout_hbm, bout_ref), (cnt_hbm, cnt_ref),
            )
        )
    ]
    icopy = pltpu.make_async_copy(ids_hbm, ids, isem)
    xcopies = []
    for g in range(groups):
        band = pl.ds(g * GR, GR)
        xcopies.append(
            pltpu.make_async_copy(cov_hbm.at[:, band], xbuf.at[:, band], xsem.at[g])
        )
    for copy in pcopies[:3] + xcopies[:1] + pcopies[3:] + xcopies[1:] + [icopy]:
        copy.start()
    for copy in pcopies[:3]:
        copy.wait()

    sub = lax.broadcasted_iota(jnp.int32, (8, 128), 0)
    lane = lax.broadcasted_iota(jnp.int32, (8, 128), 1)

    bias = bin_ref[...] * 0.5
    b0 = bias.astype(jnp.bfloat16).astype(jnp.float32)
    b1 = (bias - b0).astype(jnp.bfloat16).astype(jnp.float32)
    b2 = bias - b0 - b1
    params = jnp.concatenate(
        [win_ref[...].astype(jnp.float32) * 0.5, b0, b1, b2, jnp.zeros_like(b0)], axis=0
    )
    kx = kdim + GR
    src = lax.broadcasted_iota(jnp.int32, (16, kx), 0)
    dst = lax.broadcasted_iota(jnp.int32, (16, kx), 1)
    pick = jnp.where(dst < kdim, dst // GR, dst - kdim + cov_n) == src
    spread = lax.dot_general(
        params.astype(jnp.bfloat16),
        pick.astype(jnp.bfloat16),
        (((0,), (0,)), ((), ())),
        preferred_element_type=jnp.float32,
    )
    drow = lax.broadcasted_iota(jnp.int32, (GR, kx), 0)
    dcol = lax.broadcasted_iota(jnp.int32, (GR, kx), 1)
    diag = (dcol >= kdim) | (dcol % GR == drow)
    plane = jnp.sum(params * wvec_ref[...], axis=1, keepdims=True)
    p0 = plane.astype(jnp.bfloat16).astype(jnp.float32)
    p1 = (plane - p0).astype(jnp.bfloat16).astype(jnp.float32)
    p2 = plane - p0 - p1
    slot = lax.broadcasted_iota(jnp.int32, (16, 128), 1)
    parts = jnp.where(slot == 0, p0, jnp.where(slot == 1, p1, jnp.where(slot == 2, p2, 0.0)))
    spread_lin = lax.dot_general(
        parts.astype(jnp.bfloat16),
        pick.astype(jnp.bfloat16),
        (((0,), (0,)), ((), ())),
        preferred_element_type=jnp.float32,
    )
    for h in range(hid + LIN):
        row = spread[h : h + 1, :] if h < hid else spread_lin[h - hid : h - hid + 1, :]
        row = jnp.broadcast_to(row, (GR, kx))
        lbuf[h * GR : (h + 1) * GR, :] = jnp.where(diag, row, 0.0).astype(jnp.bfloat16)

    ones = jnp.ones((GR, cols), jnp.bfloat16)

    def network(g):
        x = xbuf[:, g * GR : (g + 1) * GR, :].reshape(kdim, cols)
        x = jnp.concatenate([x, ones], axis=0)

        v = jnp.dot(lbuf[...], x, preferred_element_type=jnp.float32)
        score = v[(hid + 2) * GR :, :] + v[(hid + 1) * GR : (hid + 2) * GR, :]
        score = score + v[hid * GR : (hid + 1) * GR, :]
        for h in range(hid):
            u = v[h * GR : (h + 1) * GR, :]
            score = score + (u * jnp.tanh(u)) * wout_ref[h]
        score = score + bout_ref[...]
        y = jnp.exp(-jnp.abs(score))
        z = y / (2.0 + y)
        q = z * z
        poly = jnp.float32(1.0 / 15)
        for n in (13, 11, 9, 7, 5, 3, 1):
            poly = poly * q + jnp.float32(1.0 / n)
        halo[0, M + g * GR : M + (g + 1) * GR, 0:cols] = jnp.maximum(score, 0.0) + 2.0 * z * poly

    for copy in pcopies[3:] + xcopies:
        copy.wait()
    for g in range(groups):
        network(g)

    icopy.wait()
    halo[1, M : M + rows, 0:cols] = ids[...].astype(jnp.float32)
    home = jnp.zeros((8, 128), jnp.float32)
    mine = jnp.zeros((8, 128), jnp.float32)
    for j in range(units):
        c = j * BLK + BLK // 2
        at = ids[BLK // 2 : BLK // 2 + 1, c // 128 * 128 : c // 128 * 128 + 128]
        home = jnp.where(sub == j, at[:, c % 128 : c % 128 + 1].astype(jnp.float32), home)
        mine = jnp.where(lane == lon * units + j, cnt_ref[j].astype(jnp.float32), mine)
    cown[0] = jnp.where(sub == lat, mine, 0.0)
    cown[1] = jnp.where(lane == lat, home, 0.0)

    def far_copies(buf, send, recv):
        return [
            pltpu.make_async_remote_copy(
                src_ref=buf.at[2, 8:16],
                dst_ref=buf.at[2 - a, 8 * (1 - b) : 8 * (1 - b) + 8],
                send_sem=send.at[k],
                recv_sem=recv.at[k],
                device_id=peer(a, b),
                device_id_type=MESH,
            )
            for k, (a, b) in enumerate(FAR)
        ]

    def row_copies(src, dst, send, recv, moves):
        return [
            pltpu.make_async_remote_copy(
                src_ref=src, dst_ref=dst.at[k], send_sem=send.at[k], recv_sem=recv.at[k],
                device_id=peer(*move), device_id_type=MESH,
            )
            for k, move in enumerate(moves)
        ]

    pl.semaphore_wait(barrier, len(greet))
    hcopies = halo_copies(halo, heast, hwest, hsend, hrecv, peer, rows, cols)
    acopies = row_copies(cown, cslot_a, asend, arecv, [(d, 0) for d in range(1, lat_n)])
    for copy in hcopies + acopies:
        copy.start()

    for copy in acopies:
        copy.wait_recv()
    total = cown[...]
    for d in range(1, lat_n):
        total = total + cslot_a[d - 1]
    crow[...] = total
    bcopies = row_copies(crow, cslot_b, bsend, brecv, [(0, d) for d in range(1, lon_n)])
    for copy in bcopies:
        copy.start()

    def ring_rows(buf, r):
        order = list(range(8, 8 + units + 1)) + [7]
        return lane_rows([buf[r, s : s + 1, :] for s in order])

    def smooth(field):
        pair = field + pltpu.roll(field, 1, 0)
        down = field + pltpu.roll(pair, 1, 0) + pltpu.roll(pair, ext_rows - 2, 0)
        pair = down + pltpu.roll(down, 1, 1)
        both = down + pltpu.roll(pair, 1, 1) + pltpu.roll(pair, ext_cols - 2, 1)
        return both * jnp.float32(1.0 / 25.0)

    for copy in hcopies:
        copy.wait_recv()
    lane_x = lax.broadcasted_iota(jnp.int32, (ext_rows, 128), 1)
    row_x = lax.broadcasted_iota(jnp.int32, (ext_rows, ext_cols), 0)
    wrap = jnp.where(lane_x < 64, heast[1], hwest[1])
    keep_e = (lane_x < M) & (lon < lon_n - 1)
    keep_w = (lane_x >= 128 - M) & (lon > 0)
    wrap = jnp.where(keep_e | keep_w, wrap, -1.0)
    whole = jnp.concatenate([halo[1, :, 0:cols], wrap], axis=1)
    gone = ((row_x < M) & (lat == 0)) | ((row_x >= M + rows) & (lat == lat_n - 1))
    whole = jnp.where(gone, -1.0, whole)
    band = 2 * M

    def classed(which, picked, base, other):
        even, odd = picked
        return jnp.where(which == even, base, jnp.where(which == odd, base + 1, other))

    def home_rows(at):
        mids = []
        for j in range(units):
            c = j * BLK + BLK // 2
            mids.append(halo[1, at : at + 1, c // 128 * 128 : c // 128 * 128 + 128])
            mids[j] = mids[j][:, c % 128 : c % 128 + 1]
        east = heast[1, at : at + 1, :][:, 32:33]
        return lane_rows(mids + [east, hwest[1, at : at + 1, :][:, 96:97]])

    kinds = classed(whole, home_rows(M + BLK // 2), 0, -1)
    code[...] = kinds
    code[0:band] = classed(whole[0:band], home_rows(M // 2 - 1), 2, kinds[0:band])
    code[ext_rows - band :] = classed(
        whole[ext_rows - band :], home_rows(M + rows + M // 2), 4, kinds[ext_rows - band :]
    )
    for p in range(2):
        reach[p] = smooth(jnp.where(code[...] == p, 1.0, 0.0))

    def fold(x):
        return jnp.sum(x.reshape(x.shape[0] // 8, 8, ext_cols), axis=0)

    def census(field, k):
        kind = code[...]
        sums = [jnp.zeros((8, 128), jnp.float32)] * 7
        for p in range(2):
            near = field * reach[p]
            head, tail = near[0:band], near[ext_rows - band :]
            hkind, tkind = kind[0:band], kind[ext_rows - band :]
            parts = [fold(jnp.where(kind == p, field, 0.0))]
            for v in (p, 1 - p):
                parts.append(fold(jnp.where(hkind == 2 + v, head, 0.0)))
                parts.append(fold(jnp.where(kind == v, near, 0.0)))
                parts.append(fold(jnp.where(tkind == 4 + v, tail, 0.0)))
            for q in range(7):
                turned = pltpu.roll(parts[q], 32 if p == 0 else ext_cols - 32, 1)
                line = jnp.sum(turned, axis=0, keepdims=True)
                for t in range(tiles):
                    sums[q] = jnp.where(
                        sub == 2 * t + p, line[:, t * 128 : t * 128 + 128], sums[q]
                    )
        ebuf[k, 2, 8:16, 0:128] = jnp.broadcast_to(
            jnp.sum(sums[0], axis=1, keepdims=True), (8, 128)
        )
        links = jnp.zeros((8, 128), jnp.float32)
        for d in range(3):
            cross = sums[4 + d]
            for b, x in enumerate(
                (jnp.where(lane < 64, cross, 0.0), sums[1 + d], jnp.where(lane < 64, 0.0, cross))
            ):
                links = jnp.where(lane == 3 * d + b, jnp.sum(x, axis=1, keepdims=True), links)
        ebuf[k, 2, 8:16, 128:256] = links
        copies = far_copies(ebuf.at[k], esend.at[k], erecv.at[k])
        for copy in copies:
            copy.start()
        return copies

    lane_u = lax.broadcasted_iota(jnp.int32, (24, 128), 1)

    def solve(k):
        first = [cbuf[r] / ebuf[k, r, :, 0:128] for r in range(5)]
        for r in range(1, 4):
            fbuf[2 * k, r - 1] = first[r]
            mix = jnp.zeros((24, 128), jnp.float32)
            for a in range(3):
                for b in range(3):
                    f = first[r + a - 1]
                    f = f if b == 1 else pltpu.roll(f, 1 if b == 0 else 23, 0)
                    mix = jnp.where(lane_u == 3 * a + b, f, mix)
            second = jnp.sum(mix * ebuf[k, r, :, 128:256], axis=1, keepdims=True)
            fbuf[2 * k + 1, r - 1] = cbuf[r] / second

    def scaled(field, i):
        kind = code[...]
        rows_f = [ring_rows(fbuf.at[i], r) for r in range(3)]

        def chosen(which, base, picked, other):
            return jnp.where(
                which == base, picked[0], jnp.where(which == base + 1, picked[1], other)
            )

        fac = chosen(kind, 0, rows_f[1], 0.0)
        head = chosen(kind[0:band], 2, rows_f[0], fac[0:band])
        tail = chosen(kind[ext_rows - band :], 4, rows_f[2], fac[ext_rows - band :])
        fac = jnp.concatenate([head, fac[band : ext_rows - band], tail], axis=0)
        return field * fac

    wrap = jnp.where(lane_x < 64, heast[0], hwest[0])
    sbuf[...] = jnp.concatenate([halo[0, :, 0:cols], wrap], axis=1)
    pending = census(sbuf[...], 0)

    for copy in bcopies:
        copy.wait_recv()
    table = crow[0]
    for d in range(1, lon_n):
        table = table + cslot_b[d - 1, 0]
    uid = jnp.where(lane < units * lon_n, sub * (units * lon_n) + lane, -1).astype(jnp.float32)
    columns = (cslot_b[0, 1], crow[1], cslot_b[lon_n - 2, 1])
    for i in range(5):
        at = lax.rem(lat + (i - 2 + lat_n), lat_n)
        for b in range(3):
            homes[i, 8 * b : 8 * b + 8, :] = jnp.broadcast_to(
                jnp.sum(jnp.where(lane == at, columns[b], 0.0), axis=1, keepdims=True), (8, 128)
            )

    def look(r, carry):
        found = [jnp.zeros((8, 128), jnp.float32)] * 3
        for s in range(6, 10 + units):
            hit = jnp.where(uid == homes[r, s : s + 1, :], table, 0.0)
            hit = jnp.sum(hit, axis=0, keepdims=True)
            found[s // 8] = jnp.where(sub == s % 8, hit, found[s // 8])
        for i in range(3):
            cbuf[r, 8 * i : 8 * i + 8, :] = jnp.broadcast_to(
                jnp.sum(found[i], axis=1, keepdims=True), (8, 128)
            )
        return carry

    lax.fori_loop(0, 5, look, 0)

    for k in range((ROUNDS + 1) // 2):
        if k > 0:
            pending = census(sbuf[...], k)
        for copy in pending:
            copy.wait_recv()
        solve(k)
        sbuf[...] = smooth(scaled(sbuf[...], 2 * k))
        if 2 * k + 1 < ROUNDS:
            sbuf[...] = smooth(scaled(sbuf[...], 2 * k + 1))
        if k == 0:
            sent = pending
    out_ref[...] = scaled(sbuf[...], ROUNDS)[M : M + rows, 0:cols]

    for copy in hcopies + acopies + bcopies + sent + pending:
        copy.wait_send()


def shards(covariates, w_in, b_in, w_out, b_out, unit_ids, unit_counts):
    lat_n = lax.axis_size("lat")
    lon_n = lax.axis_size("lon")
    cov_n, rows, cols = covariates.shape
    hid = w_in.shape[1]
    ext_rows, ext_cols = rows + 2 * M, cols + 128
    kx = cov_n * GR + GR
    f32, i32, bf16 = jnp.float32, jnp.int32, jnp.bfloat16
    hbm = pl.BlockSpec(memory_space=pltpu.HBM)
    dma = pltpu.SemaphoreType.DMA
    pairs = (ROUNDS + 1) // 2
    far = len(FAR)
    return pl.pallas_call(
        functools.partial(kernel, lat_n, lon_n),
        out_shape=pltpu.VMEM((rows, cols), f32),
        in_specs=[hbm] * 8,
        out_specs=pl.BlockSpec(memory_space=pltpu.VMEM),
        scratch_shapes=[
            pltpu.VMEM((cov_n, rows, cols), bf16),
            pltpu.VMEM((cov_n, hid), bf16),
            pltpu.VMEM((1, hid), f32),
            pltpu.VMEM((1, hid), f32),
            pltpu.SMEM((hid,), f32),
            pltpu.VMEM((1, 1), f32),
            pltpu.SMEM((unit_counts.shape[0],), i32),
            pltpu.VMEM(((hid + LIN) * GR, kx), bf16),
            pltpu.VMEM((rows, cols), i32),
            pltpu.VMEM((2, ext_rows, ext_cols), f32),
            pltpu.VMEM((2, ext_rows, 128), f32),
            pltpu.VMEM((2, ext_rows, 128), f32),
            pltpu.VMEM((ext_rows, ext_cols), i32),
            pltpu.VMEM((ext_rows, ext_cols), f32),
            pltpu.VMEM((2, ext_rows, ext_cols), f32),
            pltpu.VMEM((5, 24, 128), f32),
            pltpu.VMEM((2, 8, 128), f32),
            pltpu.VMEM((2, 8, 128), f32),
            pltpu.VMEM((lat_n - 1, 2, 8, 128), f32),
            pltpu.VMEM((lon_n - 1, 2, 8, 128), f32),
            pltpu.VMEM((5, 24, 128), f32),
            pltpu.VMEM((pairs, 5, 24, 256), f32),
            pltpu.VMEM((2 * pairs, 3, 24, 128), f32),
            dma((rows // GR,)),
            dma((6,)),
            dma(()),
            dma((8,)),
            dma((8,)),
            dma((lat_n - 1,)),
            dma((lat_n - 1,)),
            dma((lon_n - 1,)),
            dma((lon_n - 1,)),
            dma((pairs, far)),
            dma((pairs, far)),
        ],
        compiler_params=pltpu.CompilerParams(
            collective_id=0, has_side_effects=True, vmem_limit_bytes=60 * 1024 * 1024
        ),
    )(covariates, w_in, b_in.reshape(1, hid), w_out.reshape(1, hid), w_out, b_out.reshape(1, 1), unit_ids, unit_counts)


def solution(mesh):
    return jax.shard_map(
        shards,
        mesh=mesh,
        in_specs=(P(None, "lat", "lon"), P(), P(), P(), P(), P("lat", "lon"), P(("lat", "lon"))),
        out_specs=P("lat", "lon"),
        check_vma=False,
    )
```

```python
import functools

import jax
import jax.numpy as jnp
from jax import lax
from jax.experimental import pallas as pl
from jax.experimental.pallas import tpu as pltpu
from jax.sharding import PartitionSpec as P

BLK = 64
ROUNDS = 3
M = 8
GR = 16
LIN = 3
MESH = pl.DeviceIdType.MESH
DIRS = ((-1, 1), (-1, -1), (1, 1), (1, -1), (0, 1), (0, -1), (-1, 0), (1, 0))


FAR = tuple((a, b) for b in (-1, 1, 0) for a in (-2, 2, -1, 1, 0) if (a, b) != (0, 0))


def turn(x, lanes):
    lanes = lanes % 128
    return x if lanes == 0 else pltpu.roll(x, lanes, 1)


def lane_rows(units):
    lane = lax.broadcasted_iota(jnp.int32, (1, 128), 1)
    n = len(units)
    even = [jnp.where(lane < 96, units[t], units[(t + 2) % n]) for t in range(0, n, 2)]
    odd = [jnp.where(lane < 32, units[t - 1], units[t + 1]) for t in range(0, n, 2)]
    return jnp.concatenate(even, axis=1), jnp.concatenate(odd, axis=1)


def kernel(
    lat_n, lon_n, cov_hbm, win_hbm, bin_hbm, wvec_hbm, wout_hbm, bout_hbm, ids_hbm, cnt_hbm, out_ref,
    xbuf, win_ref, bin_ref, wvec_ref, wout_ref, bout_ref, cnt_ref, lbuf, ids, halo, strips, sides,
    code, sbuf, reach, homes, cown, crow, cslot_a, cslot_b, cbuf, ebuf, fbuf,
    xsem, psem, isem, hsend, hrecv, asend, arecv, bsend, brecv, esend, erecv,
):
    cov_n, rows, cols = cov_hbm.shape
    hid = win_ref.shape[1]
    kdim = cov_n * GR
    groups = rows // GR
    ext_rows, ext_cols = rows + 2 * M, cols + 128
    units = cols // BLK
    tiles = cols // 128
    lat = lax.axis_index("lat")
    lon = lax.axis_index("lon")

    def peer(dlat, dlon):
        return (lax.rem(lat + (dlat + lat_n), lat_n), lax.rem(lon + (dlon + lon_n), lon_n))

    pcopies = [
        pltpu.make_async_copy(src, dst, psem.at[k])
        for k, (src, dst) in enumerate(
            (
                (win_hbm, win_ref), (bin_hbm, bin_ref), (wvec_hbm, wvec_ref),
                (wout_hbm, wout_ref), (bout_hbm, bout_ref), (cnt_hbm, cnt_ref),
            )
        )
    ]
    icopy = pltpu.make_async_copy(ids_hbm, ids, isem)
    xcopy = pltpu.make_async_copy(cov_hbm, xbuf, xsem)
    for copy in pcopies[:3] + [xcopy]:
        copy.start()
    barrier = pltpu.get_barrier_semaphore()
    greet = [(a, b) for a, b in FAR if a != 0 and b != 0]
    greet += [(0, d) for d in range(1, lon_n)] + [(d, 0) for d in range(1, lat_n)]
    for move in greet:
        pl.semaphore_signal(barrier, inc=1, device_id=peer(*move), device_id_type=MESH)

    for copy in [icopy] + pcopies[3:]:
        copy.start()
    for copy in pcopies[:3]:
        copy.wait()

    sub = lax.broadcasted_iota(jnp.int32, (8, 128), 0)
    lane = lax.broadcasted_iota(jnp.int32, (8, 128), 1)

    bias = bin_ref[...] * 0.5
    b0 = bias.astype(jnp.bfloat16).astype(jnp.float32)
    b1 = (bias - b0).astype(jnp.bfloat16).astype(jnp.float32)
    b2 = bias - b0 - b1
    params = jnp.concatenate(
        [win_ref[...].astype(jnp.float32) * 0.5, b0, b1, b2, jnp.zeros_like(b0)], axis=0
    )
    kx = kdim + GR
    src = lax.broadcasted_iota(jnp.int32, (16, kx), 0)
    dst = lax.broadcasted_iota(jnp.int32, (16, kx), 1)
    pick = jnp.where(dst < kdim, dst // GR, dst - kdim + cov_n) == src
    spread = lax.dot_general(
        params.astype(jnp.bfloat16),
        pick.astype(jnp.bfloat16),
        (((0,), (0,)), ((), ())),
        preferred_element_type=jnp.float32,
    )
    drow = lax.broadcasted_iota(jnp.int32, (GR, kx), 0)
    dcol = lax.broadcasted_iota(jnp.int32, (GR, kx), 1)
    diag = (dcol >= kdim) | (dcol % GR == drow)
    plane = jnp.sum(params * wvec_ref[...], axis=1, keepdims=True)
    p0 = plane.astype(jnp.bfloat16).astype(jnp.float32)
    p1 = (plane - p0).astype(jnp.bfloat16).astype(jnp.float32)
    p2 = plane - p0 - p1
    slot = lax.broadcasted_iota(jnp.int32, (16, 128), 1)
    parts = jnp.where(slot == 0, p0, jnp.where(slot == 1, p1, jnp.where(slot == 2, p2, 0.0)))
    spread_lin = lax.dot_general(
        parts.astype(jnp.bfloat16),
        pick.astype(jnp.bfloat16),
        (((0,), (0,)), ((), ())),
        preferred_element_type=jnp.float32,
    )
    for h in range(hid + LIN):
        row = spread[h : h + 1, :] if h < hid else spread_lin[h - hid : h - hid + 1, :]
        row = jnp.broadcast_to(row, (GR, kx))
        lbuf[h * GR : (h + 1) * GR, :] = jnp.where(diag, row, 0.0).astype(jnp.bfloat16)

    ones = jnp.ones((GR, cols), jnp.bfloat16)

    def network(g):
        x = xbuf[:, g * GR : (g + 1) * GR, :].reshape(kdim, cols)
        x = jnp.concatenate([x, ones], axis=0)

        v = jnp.dot(lbuf[...], x, preferred_element_type=jnp.float32)
        score = v[(hid + 2) * GR :, :] + v[(hid + 1) * GR : (hid + 2) * GR, :]
        score = score + v[hid * GR : (hid + 1) * GR, :]
        for h in range(hid):
            u = v[h * GR : (h + 1) * GR, :]
            score = score + (u * jnp.tanh(u)) * wout_ref[h]
        score = score + bout_ref[...]
        y = jnp.exp(-jnp.abs(score))
        z = y / (2.0 + y)
        q = z * z
        poly = jnp.float32(1.0 / 15)
        for n in (13, 11, 9, 7, 5, 3, 1):
            poly = poly * q + jnp.float32(1.0 / n)
        halo[0, M + g * GR : M + (g + 1) * GR, 0:cols] = jnp.maximum(score, 0.0) + 2.0 * z * poly

    for copy in pcopies[3:] + [xcopy]:
        copy.wait()
    for g in range(groups):
        network(g)

    icopy.wait()
    halo[1, M : M + rows, 0:cols] = ids[...].astype(jnp.float32)
    last = cols - 128
    for k, (at, base) in enumerate(((last, 8), (0, 0))):
        strip = jnp.zeros((8, 128), jnp.float32)
        for plane in range(2):
            for i in range(rows // 8):
                spot = 64 * plane + 8 * i
                piece = halo[plane, M + 8 * i : M + 8 * i + 8, at : at + 128]
                strip = jnp.where(lane // 8 == spot // 8, turn(piece, spot + base), strip)
        strips[4 + k] = strip
    for k, at in enumerate((M, rows)):
        for b, start in enumerate((last, 0)):
            near = halo[0, at : at + 8, start : start + 128]
            mark = turn(halo[1, at : at + 8, start : start + 128], 64)
            strips[2 * k + b] = jnp.where((lane < 64) == (b == 1), near, mark)
    home = jnp.zeros((8, 128), jnp.float32)
    mine = jnp.zeros((8, 128), jnp.float32)
    for j in range(units):
        c = j * BLK + BLK // 2
        at = ids[BLK // 2 : BLK // 2 + 1, c // 128 * 128 : c // 128 * 128 + 128]
        home = jnp.where(sub == j, at[:, c % 128 : c % 128 + 1].astype(jnp.float32), home)
        mine = jnp.where(lane == lon * units + j, cnt_ref[j].astype(jnp.float32), mine)
    cown[0] = jnp.where(sub == lat, mine, 0.0)
    cown[1] = jnp.where(lane == lat, home, 0.0)

    def far_copies(buf, send, recv):
        return [
            pltpu.make_async_remote_copy(
                src_ref=buf.at[2, 8:16],
                dst_ref=buf.at[2 - a, 8 * (1 - b) : 8 * (1 - b) + 8],
                send_sem=send.at[k],
                recv_sem=recv.at[k],
                device_id=peer(a, b),
                device_id_type=MESH,
            )
            for k, (a, b) in enumerate(FAR)
        ]

    def row_copies(src, dst, send, recv, moves):
        return [
            pltpu.make_async_remote_copy(
                src_ref=src, dst_ref=dst.at[k], send_sem=send.at[k], recv_sem=recv.at[k],
                device_id=peer(*move), device_id_type=MESH,
            )
            for k, move in enumerate(moves)
        ]

    pl.semaphore_wait(barrier, len(greet))
    moves = [(strips.at[k], sides.at[k]) for k in range(6)]
    moves += [
        (halo.at[:, M : 2 * M, 0:cols], halo.at[:, rows + M : rows + 2 * M, 0:cols]),
        (halo.at[:, rows : rows + M, 0:cols], halo.at[:, 0:M, 0:cols]),
    ]
    hcopies = [
        pltpu.make_async_remote_copy(
            src_ref=src, dst_ref=dst, send_sem=hsend.at[k], recv_sem=hrecv.at[k],
            device_id=peer(*DIRS[k]), device_id_type=MESH,
        )
        for k, (src, dst) in enumerate(moves)
    ]
    acopies = row_copies(cown, cslot_a, asend, arecv, [(d, 0) for d in range(1, lat_n)])
    for copy in hcopies + acopies:
        copy.start()

    for copy in acopies:
        copy.wait_recv()
    total = cown[...]
    for d in range(1, lat_n):
        total = total + cslot_a[d - 1]
    crow[...] = total
    bcopies = row_copies(crow, cslot_b, bsend, brecv, [(0, d) for d in range(1, lon_n)])
    for copy in bcopies:
        copy.start()

    def ring_rows(buf, r):
        order = list(range(8, 8 + units + 1)) + [7]
        return lane_rows([buf[r, s : s + 1, :] for s in order])

    def smooth(field):
        pair = field + pltpu.roll(field, 1, 0)
        down = field + pltpu.roll(pair, 1, 0) + pltpu.roll(pair, ext_rows - 2, 0)
        pair = down + pltpu.roll(down, 1, 1)
        both = down + pltpu.roll(pair, 1, 1) + pltpu.roll(pair, ext_cols - 2, 1)
        return both * jnp.float32(1.0 / 25.0)

    for copy in hcopies:
        copy.wait_recv()
    lane_x = lax.broadcasted_iota(jnp.int32, (ext_rows, 128), 1)
    row_x = lax.broadcasted_iota(jnp.int32, (ext_rows, ext_cols), 0)
    low = lane < 64
    far_w, far_e, near_w, near_e, mid_w, mid_e = (sides[k] for k in range(6))
    wrap_w = [jnp.where(low, near_e, near_w)]
    wrap_i = [turn(jnp.where(low, near_w, near_e), 64)]
    for i in range(rows // 8):
        wrap_w.append(jnp.where(low, turn(mid_e, -8 * i), turn(mid_w, 120 - 8 * i)))
        wrap_i.append(jnp.where(low, turn(mid_e, 64 - 8 * i), turn(mid_w, 56 - 8 * i)))
    wrap_w = jnp.concatenate(wrap_w + [jnp.where(low, far_e, far_w)], axis=0)
    wrap_i = jnp.concatenate(wrap_i + [turn(jnp.where(low, far_w, far_e), 64)], axis=0)
    keep_e = (lane_x < M) & (lon < lon_n - 1)
    keep_w = (lane_x >= 128 - M) & (lon > 0)
    wrap = jnp.where(keep_e | keep_w, wrap_i, -1.0)
    whole = jnp.concatenate([halo[1, :, 0:cols], wrap], axis=1)
    gone = ((row_x < M) & (lat == 0)) | ((row_x >= M + rows) & (lat == lat_n - 1))
    whole = jnp.where(gone, -1.0, whole)
    band = 2 * M

    def classed(which, picked, base, other):
        even, odd = picked
        return jnp.where(which == even, base, jnp.where(which == odd, base + 1, other))

    def home_rows(at):
        mids = []
        for j in range(units):
            c = j * BLK + BLK // 2
            mids.append(halo[1, at : at + 1, c // 128 * 128 : c // 128 * 128 + 128])
            mids[j] = mids[j][:, c % 128 : c % 128 + 1]
        return lane_rows(mids + [wrap_i[at : at + 1, 4:5], wrap_i[at : at + 1, 123:124]])

    kinds = classed(whole, home_rows(M + BLK // 2), 0, -1)
    code[...] = kinds
    code[0:band] = classed(whole[0:band], home_rows(M // 2 - 1), 2, kinds[0:band])
    code[ext_rows - band :] = classed(
        whole[ext_rows - band :], home_rows(M + rows + M // 2), 4, kinds[ext_rows - band :]
    )
    for p in range(2):
        reach[p] = smooth(jnp.where(code[...] == p, 1.0, 0.0))

    def fold(x):
        return jnp.sum(x.reshape(x.shape[0] // 8, 8, ext_cols), axis=0)

    def census(field, k):
        kind = code[...]
        sums = [jnp.zeros((8, 128), jnp.float32)] * 7
        for p in range(2):
            near = field * reach[p]
            head, tail = near[0:band], near[ext_rows - band :]
            hkind, tkind = kind[0:band], kind[ext_rows - band :]
            parts = [fold(jnp.where(kind == p, field, 0.0))]
            for v in (p, 1 - p):
                parts.append(fold(jnp.where(hkind == 2 + v, head, 0.0)))
                parts.append(fold(jnp.where(kind == v, near, 0.0)))
                parts.append(fold(jnp.where(tkind == 4 + v, tail, 0.0)))
            for q in range(7):
                turned = pltpu.roll(parts[q], 32 if p == 0 else ext_cols - 32, 1)
                line = jnp.sum(turned, axis=0, keepdims=True)
                for t in range(tiles):
                    sums[q] = jnp.where(
                        sub == 2 * t + p, line[:, t * 128 : t * 128 + 128], sums[q]
                    )
        links = jnp.broadcast_to(jnp.sum(sums[0], axis=1, keepdims=True), (8, 128))
        for d in range(3):
            cross = sums[4 + d]
            for b, x in enumerate(
                (jnp.where(lane < 64, cross, 0.0), sums[1 + d], jnp.where(lane < 64, 0.0, cross))
            ):
                links = jnp.where(lane == 3 * d + b, jnp.sum(x, axis=1, keepdims=True), links)
        ebuf[k, 2, 8:16, :] = links
        copies = far_copies(ebuf.at[k], esend.at[k], erecv.at[k])
        for copy in copies:
            copy.start()
        return copies

    lane_u = lax.broadcasted_iota(jnp.int32, (24, 128), 1)

    def solve(k):
        mail = [ebuf[k, r] for r in range(5)]
        first = [cbuf[r] / jnp.where(lane_u < 64, turn(mail[r], 64), mail[r]) for r in range(5)]
        for r in range(1, 4):
            fbuf[2 * k, r - 1] = first[r]
            mix = jnp.zeros((24, 128), jnp.float32)
            for a in range(3):
                for b in range(3):
                    f = first[r + a - 1]
                    f = f if b == 1 else pltpu.roll(f, 1 if b == 0 else 23, 0)
                    mix = jnp.where(lane_u == 3 * a + b, f, mix)
            second = jnp.sum(mix * mail[r], axis=1, keepdims=True)
            fbuf[2 * k + 1, r - 1] = cbuf[r] / second

    def scaled(field, i):
        kind = code[...]
        rows_f = [ring_rows(fbuf.at[i], r) for r in range(3)]

        def chosen(which, base, picked, other):
            return jnp.where(
                which == base, picked[0], jnp.where(which == base + 1, picked[1], other)
            )

        fac = chosen(kind, 0, rows_f[1], 0.0)
        head = chosen(kind[0:band], 2, rows_f[0], fac[0:band])
        tail = chosen(kind[ext_rows - band :], 4, rows_f[2], fac[ext_rows - band :])
        fac = jnp.concatenate([head, fac[band : ext_rows - band], tail], axis=0)
        return field * fac

    sbuf[...] = jnp.concatenate([halo[0, :, 0:cols], wrap_w], axis=1)
    pending = census(sbuf[...], 0)

    for copy in bcopies:
        copy.wait_recv()
    table = crow[0]
    for d in range(1, lon_n):
        table = table + cslot_b[d - 1, 0]
    uid = jnp.where(lane < units * lon_n, sub * (units * lon_n) + lane, -1).astype(jnp.float32)
    columns = (cslot_b[0, 1], crow[1], cslot_b[lon_n - 2, 1])
    for i in range(5):
        at = lax.rem(lat + (i - 2 + lat_n), lat_n)
        for b in range(3):
            homes[i, 8 * b : 8 * b + 8, :] = jnp.broadcast_to(
                jnp.sum(jnp.where(lane == at, columns[b], 0.0), axis=1, keepdims=True), (8, 128)
            )

    def look(r, carry):
        found = [jnp.zeros((8, 128), jnp.float32)] * 3
        for s in range(6, 10 + units):
            hit = jnp.where(uid == homes[r, s : s + 1, :], table, 0.0)
            hit = jnp.sum(hit, axis=0, keepdims=True)
            found[s // 8] = jnp.where(sub == s % 8, hit, found[s // 8])
        for i in range(3):
            cbuf[r, 8 * i : 8 * i + 8, :] = jnp.broadcast_to(
                jnp.sum(found[i], axis=1, keepdims=True), (8, 128)
            )
        return carry

    lax.fori_loop(0, 5, look, 0)

    for k in range((ROUNDS + 1) // 2):
        if k > 0:
            pending = census(sbuf[...], k)
        for copy in pending:
            copy.wait_recv()
        solve(k)
        sbuf[...] = smooth(scaled(sbuf[...], 2 * k))
        if 2 * k + 1 < ROUNDS:
            sbuf[...] = smooth(scaled(sbuf[...], 2 * k + 1))
        if k == 0:
            sent = pending
    out_ref[...] = scaled(sbuf[...], ROUNDS)[M : M + rows, 0:cols]

    for copy in hcopies + acopies + bcopies + sent + pending:
        copy.wait_send()


def shards(covariates, w_in, b_in, w_out, b_out, unit_ids, unit_counts):
    lat_n = lax.axis_size("lat")
    lon_n = lax.axis_size("lon")
    cov_n, rows, cols = covariates.shape
    hid = w_in.shape[1]
    ext_rows, ext_cols = rows + 2 * M, cols + 128
    kx = cov_n * GR + GR
    f32, i32, bf16 = jnp.float32, jnp.int32, jnp.bfloat16
    hbm = pl.BlockSpec(memory_space=pltpu.HBM)
    dma = pltpu.SemaphoreType.DMA
    pairs = (ROUNDS + 1) // 2
    far = len(FAR)
    return pl.pallas_call(
        functools.partial(kernel, lat_n, lon_n),
        out_shape=pltpu.VMEM((rows, cols), f32),
        in_specs=[hbm] * 8,
        out_specs=pl.BlockSpec(memory_space=pltpu.VMEM),
        scratch_shapes=[
            pltpu.VMEM((cov_n, rows, cols), bf16),
            pltpu.VMEM((cov_n, hid), bf16),
            pltpu.VMEM((1, hid), f32),
            pltpu.VMEM((1, hid), f32),
            pltpu.SMEM((hid,), f32),
            pltpu.VMEM((1, 1), f32),
            pltpu.SMEM((unit_counts.shape[0],), i32),
            pltpu.VMEM(((hid + LIN) * GR, kx), bf16),
            pltpu.VMEM((rows, cols), i32),
            pltpu.VMEM((2, ext_rows, ext_cols), f32),
            pltpu.VMEM((6, 8, 128), f32),
            pltpu.VMEM((6, 8, 128), f32),
            pltpu.VMEM((ext_rows, ext_cols), i32),
            pltpu.VMEM((ext_rows, ext_cols), f32),
            pltpu.VMEM((2, ext_rows, ext_cols), f32),
            pltpu.VMEM((5, 24, 128), f32),
            pltpu.VMEM((2, 8, 128), f32),
            pltpu.VMEM((2, 8, 128), f32),
            pltpu.VMEM((lat_n - 1, 2, 8, 128), f32),
            pltpu.VMEM((lon_n - 1, 2, 8, 128), f32),
            pltpu.VMEM((5, 24, 128), f32),
            pltpu.VMEM((pairs, 5, 24, 128), f32),
            pltpu.VMEM((2 * pairs, 3, 24, 128), f32),
            dma(()),
            dma((6,)),
            dma(()),
            dma((8,)),
            dma((8,)),
            dma((lat_n - 1,)),
            dma((lat_n - 1,)),
            dma((lon_n - 1,)),
            dma((lon_n - 1,)),
            dma((pairs, far)),
            dma((pairs, far)),
        ],
        compiler_params=pltpu.CompilerParams(
            collective_id=0, has_side_effects=True, vmem_limit_bytes=60 * 1024 * 1024
        ),
    )(covariates, w_in, b_in.reshape(1, hid), w_out.reshape(1, hid), w_out, b_out.reshape(1, 1), unit_ids, unit_counts)


def solution(mesh):
    return jax.shard_map(
        shards,
        mesh=mesh,
        in_specs=(P(None, "lat", "lon"), P(), P(), P(), P(), P("lat", "lon"), P(("lat", "lon"))),
        out_specs=P("lat", "lon"),
        check_vma=False,
    )
```

```python
import functools

import jax
import jax.numpy as jnp
from jax import lax
from jax.experimental import pallas as pl
from jax.experimental.pallas import tpu as pltpu
from jax.sharding import PartitionSpec as P

BLK = 64
ROUNDS = 3
M = 8
GR = 16
LIN = 3
MESH = pl.DeviceIdType.MESH
DIRS = ((-1, 1), (-1, -1), (1, 1), (1, -1), (0, 1), (0, -1), (-1, 0), (1, 0))


FAR = tuple((a, b) for b in (-1, 1, 0) for a in (-2, 2, -1, 1, 0) if (a, b) != (0, 0))


def turn(x, lanes):
    lanes = lanes % 128
    return x if lanes == 0 else pltpu.roll(x, lanes, 1)


def lane_rows(units):
    lane = lax.broadcasted_iota(jnp.int32, (1, 128), 1)
    n = len(units)
    even = [jnp.where(lane < 96, units[t], units[(t + 2) % n]) for t in range(0, n, 2)]
    odd = [jnp.where(lane < 32, units[t - 1], units[t + 1]) for t in range(0, n, 2)]
    return jnp.concatenate(even, axis=1), jnp.concatenate(odd, axis=1)


def kernel(
    lat_n, lon_n, cov_hbm, win_hbm, bin_hbm, wvec_hbm, wout_hbm, bout_hbm, ids_hbm, cnt_hbm, out_ref,
    xbuf, win_ref, bin_ref, wvec_ref, wout_ref, bout_ref, cnt_ref, lbuf, ids, halo, strips, sides,
    code, sbuf, reach, homes, cown, crow, cslot_a, cslot_b, cbuf, ebuf, fbuf,
    xsem, psem, isem, hsend, hrecv, asend, arecv, bsend, brecv, esend, erecv,
):
    cov_n, rows, cols = cov_hbm.shape
    hid = win_ref.shape[1]
    kdim = cov_n * GR
    groups = rows // GR
    ext_rows, ext_cols = rows + 2 * M, cols + 128
    units = cols // BLK
    tiles = cols // 128
    lat = lax.axis_index("lat")
    lon = lax.axis_index("lon")

    def peer(dlat, dlon):
        return (lax.rem(lat + (dlat + lat_n), lat_n), lax.rem(lon + (dlon + lon_n), lon_n))

    pcopies = [
        pltpu.make_async_copy(src, dst, psem.at[k])
        for k, (src, dst) in enumerate(
            (
                (win_hbm, win_ref), (bin_hbm, bin_ref), (wvec_hbm, wvec_ref),
                (wout_hbm, wout_ref), (bout_hbm, bout_ref), (cnt_hbm, cnt_ref),
            )
        )
    ]
    icopy = pltpu.make_async_copy(ids_hbm, ids, isem)
    xcopy = pltpu.make_async_copy(cov_hbm, xbuf, xsem)
    for copy in pcopies[:3] + [xcopy]:
        copy.start()
    barrier = pltpu.get_barrier_semaphore()
    greet = [(a, b) for a, b in FAR if a != 0 and b != 0]
    greet += [(0, d) for d in range(1, lon_n)] + [(d, 0) for d in range(1, lat_n)]
    for move in greet:
        pl.semaphore_signal(barrier, inc=1, device_id=peer(*move), device_id_type=MESH)

    for copy in [icopy] + pcopies[3:]:
        copy.start()
    for copy in pcopies[:3]:
        copy.wait()

    sub = lax.broadcasted_iota(jnp.int32, (8, 128), 0)
    lane = lax.broadcasted_iota(jnp.int32, (8, 128), 1)

    bias = bin_ref[...] * 0.5
    b0 = bias.astype(jnp.bfloat16).astype(jnp.float32)
    b1 = (bias - b0).astype(jnp.bfloat16).astype(jnp.float32)
    b2 = bias - b0 - b1
    params = jnp.concatenate(
        [win_ref[...].astype(jnp.float32) * 0.5, b0, b1, b2, jnp.zeros_like(b0)], axis=0
    )
    kx = kdim + GR
    src = lax.broadcasted_iota(jnp.int32, (16, kx), 0)
    dst = lax.broadcasted_iota(jnp.int32, (16, kx), 1)
    pick = jnp.where(dst < kdim, dst // GR, dst - kdim + cov_n) == src
    spread = lax.dot_general(
        params.astype(jnp.bfloat16),
        pick.astype(jnp.bfloat16),
        (((0,), (0,)), ((), ())),
        preferred_element_type=jnp.float32,
    )
    drow = lax.broadcasted_iota(jnp.int32, (GR, kx), 0)
    dcol = lax.broadcasted_iota(jnp.int32, (GR, kx), 1)
    diag = (dcol >= kdim) | (dcol % GR == drow)
    plane = jnp.sum(params * wvec_ref[...], axis=1, keepdims=True)
    p0 = plane.astype(jnp.bfloat16).astype(jnp.float32)
    p1 = (plane - p0).astype(jnp.bfloat16).astype(jnp.float32)
    p2 = plane - p0 - p1
    slot = lax.broadcasted_iota(jnp.int32, (16, 128), 1)
    parts = jnp.where(slot == 0, p0, jnp.where(slot == 1, p1, jnp.where(slot == 2, p2, 0.0)))
    spread_lin = lax.dot_general(
        parts.astype(jnp.bfloat16),
        pick.astype(jnp.bfloat16),
        (((0,), (0,)), ((), ())),
        preferred_element_type=jnp.float32,
    )
    for h in range(hid + LIN):
        row = spread[h : h + 1, :] if h < hid else spread_lin[h - hid : h - hid + 1, :]
        row = jnp.broadcast_to(row, (GR, kx))
        lbuf[h * GR : (h + 1) * GR, :] = jnp.where(diag, row, 0.0).astype(jnp.bfloat16)

    ones = jnp.ones((GR, cols), jnp.bfloat16)

    def network(g):
        x = xbuf[:, g * GR : (g + 1) * GR, :].reshape(kdim, cols)
        x = jnp.concatenate([x, ones], axis=0)

        v = jnp.dot(lbuf[...], x, preferred_element_type=jnp.float32)
        score = v[(hid + 2) * GR :, :] + v[(hid + 1) * GR : (hid + 2) * GR, :]
        score = score + v[hid * GR : (hid + 1) * GR, :]
        for h in range(hid):
            u = v[h * GR : (h + 1) * GR, :]
            score = score + (u * jnp.tanh(u)) * wout_ref[h]
        score = score + bout_ref[...]
        y = jnp.exp(-jnp.abs(score))
        z = y / (2.0 + y)
        q = z * z
        poly = jnp.float32(1.0 / 15)
        for n in (13, 11, 9, 7, 5, 3, 1):
            poly = poly * q + jnp.float32(1.0 / n)
        halo[0, M + g * GR : M + (g + 1) * GR, 0:cols] = jnp.maximum(score, 0.0) + 2.0 * z * poly

    for copy in pcopies[3:] + [xcopy]:
        copy.wait()
    for g in range(groups):
        network(g)

    icopy.wait()
    halo[1, M : M + rows, 0:cols] = ids[...].astype(jnp.float32)
    last = cols - 128
    for k, (at, base) in enumerate(((last, 8), (0, 0))):
        strip = jnp.zeros((8, 128), jnp.float32)
        for plane in range(2):
            for i in range(rows // 8):
                spot = 64 * plane + 8 * i
                piece = halo[plane, M + 8 * i : M + 8 * i + 8, at : at + 128]
                strip = jnp.where(lane // 8 == spot // 8, turn(piece, spot + base), strip)
        strips[4 + k] = strip
    for k, at in enumerate((M, rows)):
        for b, start in enumerate((last, 0)):
            near = halo[0, at : at + 8, start : start + 128]
            mark = turn(halo[1, at : at + 8, start : start + 128], 64)
            strips[2 * k + b] = jnp.where((lane < 64) == (b == 1), near, mark)
    home = jnp.zeros((8, 128), jnp.float32)
    mine = jnp.zeros((8, 128), jnp.float32)
    for j in range(units):
        c = j * BLK + BLK // 2
        at = ids[BLK // 2 : BLK // 2 + 1, c // 128 * 128 : c // 128 * 128 + 128]
        home = jnp.where(sub == j, at[:, c % 128 : c % 128 + 1].astype(jnp.float32), home)
        mine = jnp.where(lane == lon * units + j, cnt_ref[j].astype(jnp.float32), mine)
    cown[0] = jnp.where(sub == lat, mine, 0.0)
    cown[1] = jnp.where(lane == lat, home, 0.0)

    def far_copies(buf, send, recv):
        return [
            pltpu.make_async_remote_copy(
                src_ref=buf.at[2, 8:16],
                dst_ref=buf.at[2 - a, 8 * (1 - b) : 8 * (1 - b) + 8],
                send_sem=send.at[k],
                recv_sem=recv.at[k],
                device_id=peer(a, b),
                device_id_type=MESH,
            )
            for k, (a, b) in enumerate(FAR)
        ]

    def row_copies(src, dst, send, recv, moves):
        return [
            pltpu.make_async_remote_copy(
                src_ref=src, dst_ref=dst.at[k], send_sem=send.at[k], recv_sem=recv.at[k],
                device_id=peer(*move), device_id_type=MESH,
            )
            for k, move in enumerate(moves)
        ]

    pl.semaphore_wait(barrier, len(greet))
    moves = [(strips.at[k], sides.at[k]) for k in range(6)]
    moves += [
        (halo.at[:, M : 2 * M, 0:cols], halo.at[:, rows + M : rows + 2 * M, 0:cols]),
        (halo.at[:, rows : rows + M, 0:cols], halo.at[:, 0:M, 0:cols]),
    ]
    hcopies = [
        pltpu.make_async_remote_copy(
            src_ref=src, dst_ref=dst, send_sem=hsend.at[k], recv_sem=hrecv.at[k],
            device_id=peer(*DIRS[k]), device_id_type=MESH,
        )
        for k, (src, dst) in enumerate(moves)
    ]
    acopies = row_copies(cown, cslot_a, asend, arecv, [(d, 0) for d in range(1, lat_n)])
    for copy in hcopies + acopies:
        copy.start()

    for copy in acopies:
        copy.wait_recv()
    total = cown[...]
    for d in range(1, lat_n):
        total = total + cslot_a[d - 1]
    crow[...] = total
    bcopies = row_copies(crow, cslot_b, bsend, brecv, [(0, d) for d in range(1, lon_n)])
    for copy in bcopies:
        copy.start()

    def ring_rows(buf, r):
        order = list(range(8, 8 + units + 1)) + [7]
        return lane_rows([buf[r, s : s + 1, :] for s in order])

    def smooth(field):
        pair = field + pltpu.roll(field, 1, 0)
        down = field + pltpu.roll(pair, 1, 0) + pltpu.roll(pair, ext_rows - 2, 0)
        pair = down + pltpu.roll(down, 1, 1)
        both = down + pltpu.roll(pair, 1, 1) + pltpu.roll(pair, ext_cols - 2, 1)
        return both * jnp.float32(1.0 / 25.0)

    for copy in hcopies:
        copy.wait_recv()
    lane_x = lax.broadcasted_iota(jnp.int32, (ext_rows, 128), 1)
    row_x = lax.broadcasted_iota(jnp.int32, (ext_rows, ext_cols), 0)
    low = lane < 64
    far_w, far_e, near_w, near_e, mid_w, mid_e = (sides[k] for k in range(6))
    wrap_w = [jnp.where(low, near_e, near_w)]
    wrap_i = [turn(jnp.where(low, near_w, near_e), 64)]
    for i in range(rows // 8):
        wrap_w.append(jnp.where(low, turn(mid_e, -8 * i), turn(mid_w, 120 - 8 * i)))
        wrap_i.append(jnp.where(low, turn(mid_e, 64 - 8 * i), turn(mid_w, 56 - 8 * i)))
    wrap_w = jnp.concatenate(wrap_w + [jnp.where(low, far_e, far_w)], axis=0)
    wrap_i = jnp.concatenate(wrap_i + [turn(jnp.where(low, far_w, far_e), 64)], axis=0)
    keep_e = (lane_x < M) & (lon < lon_n - 1)
    keep_w = (lane_x >= 128 - M) & (lon > 0)
    wrap = jnp.where(keep_e | keep_w, wrap_i, -1.0)
    whole = jnp.concatenate([halo[1, :, 0:cols], wrap], axis=1)
    gone = ((row_x < M) & (lat == 0)) | ((row_x >= M + rows) & (lat == lat_n - 1))
    whole = jnp.where(gone, -1.0, whole)
    band = 2 * M

    def classed(which, picked, base, other):
        even, odd = picked
        return jnp.where(which == even, base, jnp.where(which == odd, base + 1, other))

    def home_rows(at):
        mids = []
        for j in range(units):
            c = j * BLK + BLK // 2
            mids.append(halo[1, at : at + 1, c // 128 * 128 : c // 128 * 128 + 128])
            mids[j] = mids[j][:, c % 128 : c % 128 + 1]
        return lane_rows(mids + [wrap_i[at : at + 1, 4:5], wrap_i[at : at + 1, 123:124]])

    kinds = classed(whole, home_rows(M + BLK // 2), 0, -1)
    code[...] = kinds
    code[0:band] = classed(whole[0:band], home_rows(M // 2 - 1), 2, kinds[0:band])
    code[ext_rows - band :] = classed(
        whole[ext_rows - band :], home_rows(M + rows + M // 2), 4, kinds[ext_rows - band :]
    )
    for p in range(2):
        reach[p] = smooth(jnp.where(code[...] == p, 1.0, 0.0))

    def fold(x):
        return jnp.sum(x.reshape(x.shape[0] // 8, 8, ext_cols), axis=0)

    def census(field, k):
        kind = code[...]
        both = []
        for p in range(2):
            near = field * reach[p]
            head, tail = near[0:band], near[ext_rows - band :]
            hkind, tkind = kind[0:band], kind[ext_rows - band :]
            parts = [fold(jnp.where(kind == p, field, 0.0))]
            for v in (p, 1 - p):
                parts.append(fold(jnp.where(hkind == 2 + v, head, 0.0)))
                parts.append(fold(jnp.where(kind == v, near, 0.0)))
                parts.append(fold(jnp.where(tkind == 4 + v, tail, 0.0)))
            both.append(parts)
        sums = []
        for q in range(7):
            even, odd = (
                [both[p][q][:, 128 * t : 128 * t + 128] for t in range(tiles + 1)] for p in range(2)
            )
            level = []
            for t in range(tiles):
                level.append(jnp.where(lane < 96, even[t], even[t - 1]))
                level.append(jnp.where(lane < 32, odd[t + 1], odd[t]))
            step = len(level) // 2
            while step:
                bit = (sub & step) == 0
                joined = []
                for i in range(step):
                    a, b = level[i], level[i + step]
                    give = jnp.where(bit, b, a)
                    up = pltpu.roll(give, 8 - step, 0)
                    if step < 4:
                        up = jnp.where(bit, up, pltpu.roll(give, step, 0))
                    joined.append(jnp.where(bit, a, b) + up)
                level = joined
                step //= 2
            sums.append(level[0])
        inner = (lane >= 32) & (lane < 96)
        left = inner == ((sub & 1) == 1)
        links = jnp.broadcast_to(jnp.sum(sums[0], axis=1, keepdims=True), (8, 128))
        for d in range(3):
            cross = sums[4 + d]
            for b, x in enumerate(
                (jnp.where(left, cross, 0.0), sums[1 + d], jnp.where(left, 0.0, cross))
            ):
                links = jnp.where(lane == 3 * d + b, jnp.sum(x, axis=1, keepdims=True), links)
        ebuf[k, 2, 8:16, :] = links
        copies = far_copies(ebuf.at[k], esend.at[k], erecv.at[k])
        for copy in copies:
            copy.start()
        return copies

    lane_u = lax.broadcasted_iota(jnp.int32, (24, 128), 1)

    def solve(k):
        mail = [ebuf[k, r] for r in range(5)]
        first = [cbuf[r] / jnp.where(lane_u < 64, turn(mail[r], 64), mail[r]) for r in range(5)]
        for r in range(1, 4):
            fbuf[2 * k, r - 1] = first[r]
            mix = jnp.zeros((24, 128), jnp.float32)
            for a in range(3):
                for b in range(3):
                    f = first[r + a - 1]
                    f = f if b == 1 else pltpu.roll(f, 1 if b == 0 else 23, 0)
                    mix = jnp.where(lane_u == 3 * a + b, f, mix)
            second = jnp.sum(mix * mail[r], axis=1, keepdims=True)
            fbuf[2 * k + 1, r - 1] = cbuf[r] / second

    def scaled(field, i):
        kind = code[...]
        rows_f = [ring_rows(fbuf.at[i], r) for r in range(3)]

        def chosen(which, base, picked, other):
            return jnp.where(
                which == base, picked[0], jnp.where(which == base + 1, picked[1], other)
            )

        fac = chosen(kind, 0, rows_f[1], 0.0)
        head = chosen(kind[0:band], 2, rows_f[0], fac[0:band])
        tail = chosen(kind[ext_rows - band :], 4, rows_f[2], fac[ext_rows - band :])
        fac = jnp.concatenate([head, fac[band : ext_rows - band], tail], axis=0)
        return field * fac

    sbuf[...] = jnp.concatenate([halo[0, :, 0:cols], wrap_w], axis=1)
    pending = census(sbuf[...], 0)

    for copy in bcopies:
        copy.wait_recv()
    table = crow[0]
    for d in range(1, lon_n):
        table = table + cslot_b[d - 1, 0]
    uid = jnp.where(lane < units * lon_n, sub * (units * lon_n) + lane, -1).astype(jnp.float32)
    columns = (cslot_b[0, 1], crow[1], cslot_b[lon_n - 2, 1])
    for i in range(5):
        at = lax.rem(lat + (i - 2 + lat_n), lat_n)
        for b in range(3):
            homes[i, 8 * b : 8 * b + 8, :] = jnp.broadcast_to(
                jnp.sum(jnp.where(lane == at, columns[b], 0.0), axis=1, keepdims=True), (8, 128)
            )

    def look(r, carry):
        found = [jnp.zeros((8, 128), jnp.float32)] * 3
        for s in range(6, 10 + units):
            hit = jnp.where(uid == homes[r, s : s + 1, :], table, 0.0)
            hit = jnp.sum(hit, axis=0, keepdims=True)
            found[s // 8] = jnp.where(sub == s % 8, hit, found[s // 8])
        for i in range(3):
            cbuf[r, 8 * i : 8 * i + 8, :] = jnp.broadcast_to(
                jnp.sum(found[i], axis=1, keepdims=True), (8, 128)
            )
        return carry

    lax.fori_loop(0, 5, look, 0)

    for k in range((ROUNDS + 1) // 2):
        if k > 0:
            pending = census(sbuf[...], k)
        for copy in pending:
            copy.wait_recv()
        solve(k)
        field = smooth(scaled(sbuf[...], 2 * k))
        if 2 * k + 1 < ROUNDS:
            sbuf[...] = smooth(scaled(field, 2 * k + 1))
            sent = pending
        else:
            out_ref[...] = scaled(field, ROUNDS)[M : M + rows, 0:cols]

    for copy in hcopies + acopies + bcopies + sent + pending:
        copy.wait_send()


def shards(covariates, w_in, b_in, w_out, b_out, unit_ids, unit_counts):
    lat_n = lax.axis_size("lat")
    lon_n = lax.axis_size("lon")
    cov_n, rows, cols = covariates.shape
    hid = w_in.shape[1]
    ext_rows, ext_cols = rows + 2 * M, cols + 128
    kx = cov_n * GR + GR
    f32, i32, bf16 = jnp.float32, jnp.int32, jnp.bfloat16
    hbm = pl.BlockSpec(memory_space=pltpu.HBM)
    dma = pltpu.SemaphoreType.DMA
    pairs = (ROUNDS + 1) // 2
    far = len(FAR)
    return pl.pallas_call(
        functools.partial(kernel, lat_n, lon_n),
        out_shape=pltpu.VMEM((rows, cols), f32),
        in_specs=[hbm] * 8,
        out_specs=pl.BlockSpec(memory_space=pltpu.VMEM),
        scratch_shapes=[
            pltpu.VMEM((cov_n, rows, cols), bf16),
            pltpu.VMEM((cov_n, hid), bf16),
            pltpu.VMEM((1, hid), f32),
            pltpu.VMEM((1, hid), f32),
            pltpu.SMEM((hid,), f32),
            pltpu.VMEM((1, 1), f32),
            pltpu.SMEM((unit_counts.shape[0],), i32),
            pltpu.VMEM(((hid + LIN) * GR, kx), bf16),
            pltpu.VMEM((rows, cols), i32),
            pltpu.VMEM((2, ext_rows, ext_cols), f32),
            pltpu.VMEM((6, 8, 128), f32),
            pltpu.VMEM((6, 8, 128), f32),
            pltpu.VMEM((ext_rows, ext_cols), i32),
            pltpu.VMEM((ext_rows, ext_cols), f32),
            pltpu.VMEM((2, ext_rows, ext_cols), f32),
            pltpu.VMEM((5, 24, 128), f32),
            pltpu.VMEM((2, 8, 128), f32),
            pltpu.VMEM((2, 8, 128), f32),
            pltpu.VMEM((lat_n - 1, 2, 8, 128), f32),
            pltpu.VMEM((lon_n - 1, 2, 8, 128), f32),
            pltpu.VMEM((5, 24, 128), f32),
            pltpu.VMEM((pairs, 5, 24, 128), f32),
            pltpu.VMEM((2 * pairs, 3, 24, 128), f32),
            dma(()),
            dma((6,)),
            dma(()),
            dma((8,)),
            dma((8,)),
            dma((lat_n - 1,)),
            dma((lat_n - 1,)),
            dma((lon_n - 1,)),
            dma((lon_n - 1,)),
            dma((pairs, far)),
            dma((pairs, far)),
        ],
        compiler_params=pltpu.CompilerParams(
            collective_id=0, has_side_effects=True, vmem_limit_bytes=60 * 1024 * 1024
        ),
    )(covariates, w_in, b_in.reshape(1, hid), w_out.reshape(1, hid), w_out, b_out.reshape(1, 1), unit_ids, unit_counts)


def solution(mesh):
    return jax.shard_map(
        shards,
        mesh=mesh,
        in_specs=(P(None, "lat", "lon"), P(), P(), P(), P(), P("lat", "lon"), P(("lat", "lon"))),
        out_specs=P("lat", "lon"),
        check_vma=False,
    )
```

```python
import functools

import jax
import jax.numpy as jnp
from jax import lax
from jax.experimental import pallas as pl
from jax.experimental.pallas import tpu as pltpu
from jax.sharding import PartitionSpec as P

BLK = 64
ROUNDS = 3
M = 8
GR = 16
LIN = 3
MESH = pl.DeviceIdType.MESH
DIRS = ((-1, 1), (-1, -1), (1, 1), (1, -1), (0, 1), (0, -1), (-1, 0), (1, 0))


FAR = tuple((a, b) for b in (-1, 1, 0) for a in (-2, 2, -1, 1, 0) if (a, b) != (0, 0))


def turn(x, lanes):
    lanes = lanes % 128
    return x if lanes == 0 else pltpu.roll(x, lanes, 1)


def lane_rows(units):
    lane = lax.broadcasted_iota(jnp.int32, (1, 128), 1)
    n = len(units)
    even = [jnp.where(lane < 96, units[t], units[(t + 2) % n]) for t in range(0, n, 2)]
    odd = [jnp.where(lane < 32, units[t - 1], units[t + 1]) for t in range(0, n, 2)]
    return jnp.concatenate(even, axis=1), jnp.concatenate(odd, axis=1)


def kernel(
    lat_n, lon_n, cov_hbm, win_hbm, bin_hbm, wvec_hbm, wout_hbm, bout_hbm, ids_hbm, cnt_hbm, out_ref,
    xbuf, win_ref, bin_ref, wvec_ref, wout_ref, bout_ref, cnt_ref, lbuf, ids, halo, strips, sides,
    code, sbuf, reach, homes, cown, crow, cslot_a, cslot_b, cbuf, ebuf, fbuf,
    xsem, psem, isem, hsend, hrecv, asend, arecv, bsend, brecv, esend, erecv,
):
    cov_n, rows, cols = cov_hbm.shape
    hid = win_ref.shape[1]
    kdim = cov_n * GR
    groups = rows // GR
    ext_rows, ext_cols = rows + 2 * M, cols + 128
    units = cols // BLK
    tiles = cols // 128
    lat = lax.axis_index("lat")
    lon = lax.axis_index("lon")

    def peer(dlat, dlon):
        return (lax.rem(lat + (dlat + lat_n), lat_n), lax.rem(lon + (dlon + lon_n), lon_n))

    pcopies = [
        pltpu.make_async_copy(src, dst, psem.at[k])
        for k, (src, dst) in enumerate(
            (
                (win_hbm, win_ref), (bin_hbm, bin_ref), (wvec_hbm, wvec_ref),
                (wout_hbm, wout_ref), (bout_hbm, bout_ref), (cnt_hbm, cnt_ref),
            )
        )
    ]
    icopy = pltpu.make_async_copy(ids_hbm, ids, isem)
    xcopy = pltpu.make_async_copy(cov_hbm, xbuf, xsem)
    for copy in pcopies[:3] + [xcopy]:
        copy.start()
    barrier = pltpu.get_barrier_semaphore()
    greet = [(a, b) for a, b in FAR if a != 0 and b != 0]
    greet += [(0, d) for d in range(1, lon_n)] + [(d, 0) for d in range(1, lat_n)]
    for move in greet:
        pl.semaphore_signal(barrier, inc=1, device_id=peer(*move), device_id_type=MESH)

    for copy in [icopy] + pcopies[3:]:
        copy.start()
    for copy in pcopies[:3]:
        copy.wait()

    sub = lax.broadcasted_iota(jnp.int32, (8, 128), 0)
    lane = lax.broadcasted_iota(jnp.int32, (8, 128), 1)

    bias = bin_ref[...] * 0.5
    b0 = bias.astype(jnp.bfloat16).astype(jnp.float32)
    b1 = (bias - b0).astype(jnp.bfloat16).astype(jnp.float32)
    b2 = bias - b0 - b1
    params = jnp.concatenate(
        [win_ref[...].astype(jnp.float32) * 0.5, b0, b1, b2, jnp.zeros_like(b0)], axis=0
    )
    kx = kdim + GR
    src = lax.broadcasted_iota(jnp.int32, (16, kx), 0)
    dst = lax.broadcasted_iota(jnp.int32, (16, kx), 1)
    pick = jnp.where(dst < kdim, dst // GR, dst - kdim + cov_n) == src
    spread = lax.dot_general(
        params.astype(jnp.bfloat16),
        pick.astype(jnp.bfloat16),
        (((0,), (0,)), ((), ())),
        preferred_element_type=jnp.float32,
    )
    drow = lax.broadcasted_iota(jnp.int32, (GR, kx), 0)
    dcol = lax.broadcasted_iota(jnp.int32, (GR, kx), 1)
    diag = (dcol >= kdim) | (dcol % GR == drow)
    plane = jnp.sum(params * wvec_ref[...], axis=1, keepdims=True)
    p0 = plane.astype(jnp.bfloat16).astype(jnp.float32)
    p1 = (plane - p0).astype(jnp.bfloat16).astype(jnp.float32)
    p2 = plane - p0 - p1
    slot = lax.broadcasted_iota(jnp.int32, (16, 128), 1)
    parts = jnp.where(slot == 0, p0, jnp.where(slot == 1, p1, jnp.where(slot == 2, p2, 0.0)))
    spread_lin = lax.dot_general(
        parts.astype(jnp.bfloat16),
        pick.astype(jnp.bfloat16),
        (((0,), (0,)), ((), ())),
        preferred_element_type=jnp.float32,
    )
    for h in range(hid + LIN):
        row = spread[h : h + 1, :] if h < hid else spread_lin[h - hid : h - hid + 1, :]
        row = jnp.broadcast_to(row, (GR, kx))
        lbuf[h * GR : (h + 1) * GR, :] = jnp.where(diag, row, 0.0).astype(jnp.bfloat16)

    ones = jnp.ones((GR, cols), jnp.bfloat16)

    def network(g):
        x = xbuf[:, g * GR : (g + 1) * GR, :].reshape(kdim, cols)
        x = jnp.concatenate([x, ones], axis=0)

        v = jnp.dot(lbuf[...], x, preferred_element_type=jnp.float32)
        score = v[(hid + 2) * GR :, :] + v[(hid + 1) * GR : (hid + 2) * GR, :]
        score = score + v[hid * GR : (hid + 1) * GR, :]
        for h in range(hid):
            u = v[h * GR : (h + 1) * GR, :]
            score = score + (u * jnp.tanh(u)) * wout_ref[h]
        score = score + bout_ref[...]
        y = jnp.exp(-jnp.abs(score))
        z = y / (2.0 + y)
        q = z * z
        poly = jnp.float32(1.0 / 15)
        for n in (13, 11, 9, 7, 5, 3, 1):
            poly = poly * q + jnp.float32(1.0 / n)
        halo[0, M + g * GR : M + (g + 1) * GR, 0:cols] = jnp.maximum(score, 0.0) + 2.0 * z * poly

    for copy in pcopies[3:] + [xcopy]:
        copy.wait()
    icopy.wait()
    halo[1, M : M + rows, 0:cols] = ids[...].astype(jnp.float32)
    home = jnp.zeros((8, 128), jnp.float32)
    mine = jnp.zeros((8, 128), jnp.float32)
    for j in range(units):
        c = j * BLK + BLK // 2
        at = ids[BLK // 2 : BLK // 2 + 1, c // 128 * 128 : c // 128 * 128 + 128]
        home = jnp.where(sub == j, at[:, c % 128 : c % 128 + 1].astype(jnp.float32), home)
        mine = jnp.where(lane == lon * units + j, cnt_ref[j].astype(jnp.float32), mine)
    cown[0] = jnp.where(sub == lat, mine, 0.0)
    cown[1] = jnp.where(lane == lat, home, 0.0)

    ends = ((cols - 128, 8), (0, 0))

    def packed(strip, plane, at, base):
        for i in range(rows // 8):
            spot = 64 * plane + 8 * i
            piece = halo[plane, M + 8 * i : M + 8 * i + 8, at : at + 128]
            strip = jnp.where(lane // 8 == spot // 8, turn(piece, spot + base), strip)
        return strip

    for k, (at, base) in enumerate(ends):
        strips[4 + k] = packed(jnp.zeros((8, 128), jnp.float32), 1, at, base)
    for k, at in enumerate((M, rows)):
        for b, (start, _) in enumerate(ends):
            strips[2 * k + b] = turn(halo[1, at : at + 8, start : start + 128], 64)

    for g in range(groups):
        network(g)


    for k, (at, base) in enumerate(ends):
        strips[4 + k] = packed(strips[4 + k], 0, at, base)
    for k, at in enumerate((M, rows)):
        for b, (start, _) in enumerate(ends):
            near = halo[0, at : at + 8, start : start + 128]
            strips[2 * k + b] = jnp.where((lane < 64) == (b == 1), near, strips[2 * k + b])

    def far_copies(buf, send, recv):
        return [
            pltpu.make_async_remote_copy(
                src_ref=buf.at[2, 8:16],
                dst_ref=buf.at[2 - a, 8 * (1 - b) : 8 * (1 - b) + 8],
                send_sem=send.at[k],
                recv_sem=recv.at[k],
                device_id=peer(a, b),
                device_id_type=MESH,
            )
            for k, (a, b) in enumerate(FAR)
        ]

    def row_copies(src, dst, send, recv, moves):
        return [
            pltpu.make_async_remote_copy(
                src_ref=src, dst_ref=dst.at[k], send_sem=send.at[k], recv_sem=recv.at[k],
                device_id=peer(*move), device_id_type=MESH,
            )
            for k, move in enumerate(moves)
        ]

    pl.semaphore_wait(barrier, len(greet))
    moves = [(strips.at[k], sides.at[k]) for k in range(6)]
    moves += [
        (halo.at[:, M : 2 * M, 0:cols], halo.at[:, rows + M : rows + 2 * M, 0:cols]),
        (halo.at[:, rows : rows + M, 0:cols], halo.at[:, 0:M, 0:cols]),
    ]
    hcopies = [
        pltpu.make_async_remote_copy(
            src_ref=src, dst_ref=dst, send_sem=hsend.at[k], recv_sem=hrecv.at[k],
            device_id=peer(*DIRS[k]), device_id_type=MESH,
        )
        for k, (src, dst) in enumerate(moves)
    ]
    acopies = row_copies(cown, cslot_a, asend, arecv, [(d, 0) for d in range(1, lat_n)])
    for copy in hcopies + acopies:
        copy.start()

    for copy in acopies:
        copy.wait_recv()
    total = cown[...]
    for d in range(1, lat_n):
        total = total + cslot_a[d - 1]
    crow[...] = total
    bcopies = row_copies(crow, cslot_b, bsend, brecv, [(0, d) for d in range(1, lon_n)])
    for copy in bcopies:
        copy.start()

    def ring_rows(buf, r):
        order = list(range(8, 8 + units + 1)) + [7]
        return lane_rows([buf[r, s : s + 1, :] for s in order])

    def smooth(field):
        pair = field + pltpu.roll(field, 1, 0)
        down = field + pltpu.roll(pair, 1, 0) + pltpu.roll(pair, ext_rows - 2, 0)
        pair = down + pltpu.roll(down, 1, 1)
        both = down + pltpu.roll(pair, 1, 1) + pltpu.roll(pair, ext_cols - 2, 1)
        return both * jnp.float32(1.0 / 25.0)

    for copy in hcopies:
        copy.wait_recv()
    lane_x = lax.broadcasted_iota(jnp.int32, (ext_rows, 128), 1)
    row_x = lax.broadcasted_iota(jnp.int32, (ext_rows, ext_cols), 0)
    low = lane < 64
    far_w, far_e, near_w, near_e, mid_w, mid_e = (sides[k] for k in range(6))
    wrap_w = [jnp.where(low, near_e, near_w)]
    wrap_i = [turn(jnp.where(low, near_w, near_e), 64)]
    for i in range(rows // 8):
        wrap_w.append(jnp.where(low, turn(mid_e, -8 * i), turn(mid_w, 120 - 8 * i)))
        wrap_i.append(jnp.where(low, turn(mid_e, 64 - 8 * i), turn(mid_w, 56 - 8 * i)))
    wrap_w = jnp.concatenate(wrap_w + [jnp.where(low, far_e, far_w)], axis=0)
    wrap_i = jnp.concatenate(wrap_i + [turn(jnp.where(low, far_w, far_e), 64)], axis=0)
    keep_e = (lane_x < M) & (lon < lon_n - 1)
    keep_w = (lane_x >= 128 - M) & (lon > 0)
    wrap = jnp.where(keep_e | keep_w, wrap_i, -1.0)
    whole = jnp.concatenate([halo[1, :, 0:cols], wrap], axis=1)
    gone = ((row_x < M) & (lat == 0)) | ((row_x >= M + rows) & (lat == lat_n - 1))
    whole = jnp.where(gone, -1.0, whole)
    band = 2 * M

    def classed(which, picked, base, other):
        even, odd = picked
        return jnp.where(which == even, base, jnp.where(which == odd, base + 1, other))

    def home_rows(at):
        mids = []
        for j in range(units):
            c = j * BLK + BLK // 2
            mids.append(halo[1, at : at + 1, c // 128 * 128 : c // 128 * 128 + 128])
            mids[j] = mids[j][:, c % 128 : c % 128 + 1]
        return lane_rows(mids + [wrap_i[at : at + 1, 4:5], wrap_i[at : at + 1, 123:124]])

    kinds = classed(whole, home_rows(M + BLK // 2), 0, -1)
    code[...] = kinds
    code[0:band] = classed(whole[0:band], home_rows(M // 2 - 1), 2, kinds[0:band])
    code[ext_rows - band :] = classed(
        whole[ext_rows - band :], home_rows(M + rows + M // 2), 4, kinds[ext_rows - band :]
    )
    for p in range(2):
        reach[p] = smooth(jnp.where(code[...] == p, 1.0, 0.0))

    def fold(x):
        return jnp.sum(x.reshape(x.shape[0] // 8, 8, ext_cols), axis=0)

    def census(field, k):
        kind = code[...]
        both = []
        for p in range(2):
            near = field * reach[p]
            head, tail = near[0:band], near[ext_rows - band :]
            hkind, tkind = kind[0:band], kind[ext_rows - band :]
            parts = [fold(jnp.where(kind == p, field, 0.0))]
            for v in (p, 1 - p):
                parts.append(fold(jnp.where(hkind == 2 + v, head, 0.0)))
                parts.append(fold(jnp.where(kind == v, near, 0.0)))
                parts.append(fold(jnp.where(tkind == 4 + v, tail, 0.0)))
            both.append(parts)
        sums = []
        for q in range(7):
            even, odd = (
                [both[p][q][:, 128 * t : 128 * t + 128] for t in range(tiles + 1)] for p in range(2)
            )
            level = []
            for t in range(tiles):
                level.append(jnp.where(lane < 96, even[t], even[t - 1]))
                level.append(jnp.where(lane < 32, odd[t + 1], odd[t]))
            step = len(level) // 2
            while step:
                bit = (sub & step) == 0
                joined = []
                for i in range(step):
                    a, b = level[i], level[i + step]
                    give = jnp.where(bit, b, a)
                    up = pltpu.roll(give, 8 - step, 0)
                    if step < 4:
                        up = jnp.where(bit, up, pltpu.roll(give, step, 0))
                    joined.append(jnp.where(bit, a, b) + up)
                level = joined
                step //= 2
            sums.append(level[0])
        inner = (lane >= 32) & (lane < 96)
        left = inner == ((sub & 1) == 1)
        links = jnp.broadcast_to(jnp.sum(sums[0], axis=1, keepdims=True), (8, 128))
        for d in range(3):
            cross = sums[4 + d]
            for b, x in enumerate(
                (jnp.where(left, cross, 0.0), sums[1 + d], jnp.where(left, 0.0, cross))
            ):
                links = jnp.where(lane == 3 * d + b, jnp.sum(x, axis=1, keepdims=True), links)
        ebuf[k, 2, 8:16, :] = links
        copies = far_copies(ebuf.at[k], esend.at[k], erecv.at[k])
        for copy in copies:
            copy.start()
        return copies

    lane_u = lax.broadcasted_iota(jnp.int32, (24, 128), 1)

    def solve(k):
        mail = [ebuf[k, r] for r in range(5)]
        first = [cbuf[r] / jnp.where(lane_u < 64, turn(mail[r], 64), mail[r]) for r in range(5)]
        for r in range(1, 4):
            fbuf[2 * k, r - 1] = first[r]
            mix = jnp.zeros((24, 128), jnp.float32)
            for a in range(3):
                for b in range(3):
                    f = first[r + a - 1]
                    f = f if b == 1 else pltpu.roll(f, 1 if b == 0 else 23, 0)
                    mix = jnp.where(lane_u == 3 * a + b, f, mix)
            second = jnp.sum(mix * mail[r], axis=1, keepdims=True)
            fbuf[2 * k + 1, r - 1] = cbuf[r] / second

    def scaled(field, i):
        kind = code[...]
        rows_f = [ring_rows(fbuf.at[i], r) for r in range(3)]

        def chosen(which, base, picked, other):
            return jnp.where(
                which == base, picked[0], jnp.where(which == base + 1, picked[1], other)
            )

        fac = chosen(kind, 0, rows_f[1], 0.0)
        head = chosen(kind[0:band], 2, rows_f[0], fac[0:band])
        tail = chosen(kind[ext_rows - band :], 4, rows_f[2], fac[ext_rows - band :])
        fac = jnp.concatenate([head, fac[band : ext_rows - band], tail], axis=0)
        return field * fac

    sbuf[...] = jnp.concatenate([halo[0, :, 0:cols], wrap_w], axis=1)
    pending = census(sbuf[...], 0)

    for copy in bcopies:
        copy.wait_recv()
    table = crow[0]
    for d in range(1, lon_n):
        table = table + cslot_b[d - 1, 0]
    uid = jnp.where(lane < units * lon_n, sub * (units * lon_n) + lane, -1).astype(jnp.float32)
    columns = (cslot_b[0, 1], crow[1], cslot_b[lon_n - 2, 1])
    for i in range(5):
        at = lax.rem(lat + (i - 2 + lat_n), lat_n)
        for b in range(3):
            homes[i, 8 * b : 8 * b + 8, :] = jnp.broadcast_to(
                jnp.sum(jnp.where(lane == at, columns[b], 0.0), axis=1, keepdims=True), (8, 128)
            )

    def look(r, carry):
        found = [jnp.zeros((8, 128), jnp.float32)] * 3
        for s in range(6, 10 + units):
            hit = jnp.where(uid == homes[r, s : s + 1, :], table, 0.0)
            hit = jnp.sum(hit, axis=0, keepdims=True)
            found[s // 8] = jnp.where(sub == s % 8, hit, found[s // 8])
        for i in range(3):
            cbuf[r, 8 * i : 8 * i + 8, :] = jnp.broadcast_to(
                jnp.sum(found[i], axis=1, keepdims=True), (8, 128)
            )
        return carry

    lax.fori_loop(0, 5, look, 0)

    for k in range((ROUNDS + 1) // 2):
        if k > 0:
            pending = census(sbuf[...], k)
        for copy in pending:
            copy.wait_recv()
        solve(k)
        field = smooth(scaled(sbuf[...], 2 * k))
        if 2 * k + 1 < ROUNDS:
            sbuf[...] = smooth(scaled(field, 2 * k + 1))
            sent = pending
        else:
            out_ref[...] = scaled(field, ROUNDS)[M : M + rows, 0:cols]

    for copy in hcopies + acopies + bcopies + sent + pending:
        copy.wait_send()


def shards(covariates, w_in, b_in, w_out, b_out, unit_ids, unit_counts):
    lat_n = lax.axis_size("lat")
    lon_n = lax.axis_size("lon")
    cov_n, rows, cols = covariates.shape
    hid = w_in.shape[1]
    ext_rows, ext_cols = rows + 2 * M, cols + 128
    kx = cov_n * GR + GR
    f32, i32, bf16 = jnp.float32, jnp.int32, jnp.bfloat16
    hbm = pl.BlockSpec(memory_space=pltpu.HBM)
    dma = pltpu.SemaphoreType.DMA
    pairs = (ROUNDS + 1) // 2
    far = len(FAR)
    return pl.pallas_call(
        functools.partial(kernel, lat_n, lon_n),
        out_shape=pltpu.VMEM((rows, cols), f32),
        in_specs=[hbm] * 8,
        out_specs=pl.BlockSpec(memory_space=pltpu.VMEM),
        scratch_shapes=[
            pltpu.VMEM((cov_n, rows, cols), bf16),
            pltpu.VMEM((cov_n, hid), bf16),
            pltpu.VMEM((1, hid), f32),
            pltpu.VMEM((1, hid), f32),
            pltpu.SMEM((hid,), f32),
            pltpu.VMEM((1, 1), f32),
            pltpu.SMEM((unit_counts.shape[0],), i32),
            pltpu.VMEM(((hid + LIN) * GR, kx), bf16),
            pltpu.VMEM((rows, cols), i32),
            pltpu.VMEM((2, ext_rows, ext_cols), f32),
            pltpu.VMEM((6, 8, 128), f32),
            pltpu.VMEM((6, 8, 128), f32),
            pltpu.VMEM((ext_rows, ext_cols), i32),
            pltpu.VMEM((ext_rows, ext_cols), f32),
            pltpu.VMEM((2, ext_rows, ext_cols), f32),
            pltpu.VMEM((5, 24, 128), f32),
            pltpu.VMEM((2, 8, 128), f32),
            pltpu.VMEM((2, 8, 128), f32),
            pltpu.VMEM((lat_n - 1, 2, 8, 128), f32),
            pltpu.VMEM((lon_n - 1, 2, 8, 128), f32),
            pltpu.VMEM((5, 24, 128), f32),
            pltpu.VMEM((pairs, 5, 24, 128), f32),
            pltpu.VMEM((2 * pairs, 3, 24, 128), f32),
            dma(()),
            dma((6,)),
            dma(()),
            dma((8,)),
            dma((8,)),
            dma((lat_n - 1,)),
            dma((lat_n - 1,)),
            dma((lon_n - 1,)),
            dma((lon_n - 1,)),
            dma((pairs, far)),
            dma((pairs, far)),
        ],
        compiler_params=pltpu.CompilerParams(
            collective_id=0, has_side_effects=True, vmem_limit_bytes=60 * 1024 * 1024
        ),
    )(covariates, w_in, b_in.reshape(1, hid), w_out.reshape(1, hid), w_out, b_out.reshape(1, 1), unit_ids, unit_counts)


def solution(mesh):
    return jax.shard_map(
        shards,
        mesh=mesh,
        in_specs=(P(None, "lat", "lon"), P(), P(), P(), P(), P("lat", "lon"), P(("lat", "lon"))),
        out_specs=P("lat", "lon"),
        check_vma=False,
    )
```

```python
import functools

import jax
import jax.numpy as jnp
from jax import lax
from jax.experimental import pallas as pl
from jax.experimental.pallas import tpu as pltpu
from jax.sharding import PartitionSpec as P

BLK = 64
ROUNDS = 3
M = 8
GR = 16
LIN = 3
MESH = pl.DeviceIdType.MESH
DIRS = ((-1, 1), (-1, -1), (1, 1), (1, -1), (0, 1), (0, -1), (-1, 0), (1, 0))


FAR = tuple((a, b) for b in (-1, 1, 0) for a in (-2, 2, -1, 1, 0) if (a, b) != (0, 0))


def turn(x, lanes):
    lanes = lanes % 128
    return x if lanes == 0 else pltpu.roll(x, lanes, 1)


def lane_rows(units):
    lane = lax.broadcasted_iota(jnp.int32, (1, 128), 1)
    n = len(units)
    even = [jnp.where(lane < 96, units[t], units[(t + 2) % n]) for t in range(0, n, 2)]
    odd = [jnp.where(lane < 32, units[t - 1], units[t + 1]) for t in range(0, n, 2)]
    return jnp.concatenate(even, axis=1), jnp.concatenate(odd, axis=1)


def kernel(
    lat_n, lon_n, cov_hbm, win_hbm, bin_hbm, wvec_hbm, wout_hbm, bout_hbm, ids_hbm, cnt_hbm, out_ref,
    xbuf, win_ref, bin_ref, wvec_ref, wout_ref, bout_ref, cnt_ref, lbuf, ids, halo, strips, sides,
    code, sbuf, reach, homes, cown, crow, cslot_a, cslot_b, cbuf, ebuf, fbuf,
    xsem, psem, isem, hsend, hrecv, asend, arecv, bsend, brecv, esend, erecv,
):
    cov_n, rows, cols = cov_hbm.shape
    hid = win_ref.shape[1]
    kdim = cov_n * GR
    groups = rows // GR
    ext_rows, ext_cols = rows + 2 * M, cols + 128
    units = cols // BLK
    tiles = cols // 128
    lat = lax.axis_index("lat")
    lon = lax.axis_index("lon")

    def peer(dlat, dlon):
        return (lax.rem(lat + (dlat + lat_n), lat_n), lax.rem(lon + (dlon + lon_n), lon_n))

    pcopies = [
        pltpu.make_async_copy(src, dst, psem.at[k])
        for k, (src, dst) in enumerate(
            (
                (win_hbm, win_ref), (bin_hbm, bin_ref), (wvec_hbm, wvec_ref),
                (wout_hbm, wout_ref), (bout_hbm, bout_ref), (cnt_hbm, cnt_ref),
            )
        )
    ]
    icopy = pltpu.make_async_copy(ids_hbm, ids, isem)
    xcopy = pltpu.make_async_copy(cov_hbm, xbuf, xsem)
    for copy in [xcopy] + pcopies[:3]:
        copy.start()
    barrier = pltpu.get_barrier_semaphore()
    greet = [(a, b) for a, b in FAR if a != 0 and b != 0]
    greet += [(0, d) for d in range(1, lon_n)] + [(d, 0) for d in range(1, lat_n)]
    for move in greet:
        pl.semaphore_signal(barrier, inc=1, device_id=peer(*move), device_id_type=MESH)

    for copy in [icopy] + pcopies[3:]:
        copy.start()
    for copy in pcopies[:3]:
        copy.wait()

    sub = lax.broadcasted_iota(jnp.int32, (8, 128), 0)
    lane = lax.broadcasted_iota(jnp.int32, (8, 128), 1)

    bias = bin_ref[...] * 0.5
    b0 = bias.astype(jnp.bfloat16).astype(jnp.float32)
    b1 = (bias - b0).astype(jnp.bfloat16).astype(jnp.float32)
    b2 = bias - b0 - b1
    params = jnp.concatenate(
        [win_ref[...].astype(jnp.float32) * 0.5, b0, b1, b2, jnp.zeros_like(b0)], axis=0
    )
    kx = kdim + GR
    src = lax.broadcasted_iota(jnp.int32, (16, kx), 0)
    dst = lax.broadcasted_iota(jnp.int32, (16, kx), 1)
    pick = jnp.where(dst < kdim, dst // GR, dst - kdim + cov_n) == src
    spread = lax.dot_general(
        params.astype(jnp.bfloat16),
        pick.astype(jnp.bfloat16),
        (((0,), (0,)), ((), ())),
        preferred_element_type=jnp.float32,
    )
    drow = lax.broadcasted_iota(jnp.int32, (GR, kx), 0)
    dcol = lax.broadcasted_iota(jnp.int32, (GR, kx), 1)
    diag = (dcol >= kdim) | (dcol % GR == drow)
    plane = jnp.sum(params * wvec_ref[...], axis=1, keepdims=True)
    p0 = plane.astype(jnp.bfloat16).astype(jnp.float32)
    p1 = (plane - p0).astype(jnp.bfloat16).astype(jnp.float32)
    p2 = plane - p0 - p1
    slot = lax.broadcasted_iota(jnp.int32, (16, 128), 1)
    parts = jnp.where(slot == 0, p0, jnp.where(slot == 1, p1, jnp.where(slot == 2, p2, 0.0)))
    spread_lin = lax.dot_general(
        parts.astype(jnp.bfloat16),
        pick.astype(jnp.bfloat16),
        (((0,), (0,)), ((), ())),
        preferred_element_type=jnp.float32,
    )
    for h in range(hid + LIN):
        row = spread[h : h + 1, :] if h < hid else spread_lin[h - hid : h - hid + 1, :]
        row = jnp.broadcast_to(row, (GR, kx))
        lbuf[h * GR : (h + 1) * GR, :] = jnp.where(diag, row, 0.0).astype(jnp.bfloat16)

    ones = jnp.ones((GR, cols), jnp.bfloat16)

    def network(g):
        x = xbuf[:, g * GR : (g + 1) * GR, :].reshape(kdim, cols)
        x = jnp.concatenate([x, ones], axis=0)

        v = jnp.dot(lbuf[...], x, preferred_element_type=jnp.float32)
        score = v[(hid + 2) * GR :, :] + v[(hid + 1) * GR : (hid + 2) * GR, :]
        score = score + v[hid * GR : (hid + 1) * GR, :]
        for h in range(hid):
            u = v[h * GR : (h + 1) * GR, :]
            score = score + (u * jnp.tanh(u)) * wout_ref[h]
        score = score + bout_ref[...]
        y = jnp.exp(-jnp.abs(score))
        z = y / (2.0 + y)
        q = z * z
        poly = jnp.float32(1.0 / 15)
        for n in (13, 11, 9, 7, 5, 3, 1):
            poly = poly * q + jnp.float32(1.0 / n)
        halo[0, M + g * GR : M + (g + 1) * GR, 0:cols] = jnp.maximum(score, 0.0) + 2.0 * z * poly

    for copy in pcopies[3:] + [xcopy]:
        copy.wait()
    icopy.wait()
    halo[1, M : M + rows, 0:cols] = ids[...].astype(jnp.float32)
    home = jnp.zeros((8, 128), jnp.float32)
    mine = jnp.zeros((8, 128), jnp.float32)
    for j in range(units):
        c = j * BLK + BLK // 2
        at = ids[BLK // 2 : BLK // 2 + 1, c // 128 * 128 : c // 128 * 128 + 128]
        home = jnp.where(sub == j, at[:, c % 128 : c % 128 + 1].astype(jnp.float32), home)
        mine = jnp.where(lane == lon * units + j, cnt_ref[j].astype(jnp.float32), mine)
    cown[0] = jnp.where(sub == lat, mine, 0.0)
    cown[1] = jnp.where(lane == lat, home, 0.0)

    ends = ((cols - 128, 8), (0, 0))

    def packed(strip, plane, at, base):
        for i in range(rows // 8):
            spot = 64 * plane + 8 * i
            piece = halo[plane, M + 8 * i : M + 8 * i + 8, at : at + 128]
            strip = jnp.where(lane // 8 == spot // 8, turn(piece, spot + base), strip)
        return strip

    for k, (at, base) in enumerate(ends):
        strips[4 + k] = packed(jnp.zeros((8, 128), jnp.float32), 1, at, base)
    for k, at in enumerate((M, rows)):
        for b, (start, _) in enumerate(ends):
            strips[2 * k + b] = turn(halo[1, at : at + 8, start : start + 128], 64)

    for g in range(groups):
        network(g)


    for k, (at, base) in enumerate(ends):
        strips[4 + k] = packed(strips[4 + k], 0, at, base)
    for k, at in enumerate((M, rows)):
        for b, (start, _) in enumerate(ends):
            near = halo[0, at : at + 8, start : start + 128]
            strips[2 * k + b] = jnp.where((lane < 64) == (b == 1), near, strips[2 * k + b])

    def far_copies(buf, send, recv):
        return [
            pltpu.make_async_remote_copy(
                src_ref=buf.at[2, 8:16],
                dst_ref=buf.at[2 - a, 8 * (1 - b) : 8 * (1 - b) + 8],
                send_sem=send.at[k],
                recv_sem=recv.at[k],
                device_id=peer(a, b),
                device_id_type=MESH,
            )
            for k, (a, b) in enumerate(FAR)
        ]

    def row_copies(src, dst, send, recv, moves):
        return [
            pltpu.make_async_remote_copy(
                src_ref=src, dst_ref=dst.at[k], send_sem=send.at[k], recv_sem=recv.at[k],
                device_id=peer(*move), device_id_type=MESH,
            )
            for k, move in enumerate(moves)
        ]

    pl.semaphore_wait(barrier, len(greet))
    moves = [(strips.at[k], sides.at[k]) for k in range(6)]
    moves += [
        (halo.at[:, M : 2 * M, 0:cols], halo.at[:, rows + M : rows + 2 * M, 0:cols]),
        (halo.at[:, rows : rows + M, 0:cols], halo.at[:, 0:M, 0:cols]),
    ]
    hcopies = [
        pltpu.make_async_remote_copy(
            src_ref=src, dst_ref=dst, send_sem=hsend.at[k], recv_sem=hrecv.at[k],
            device_id=peer(*DIRS[k]), device_id_type=MESH,
        )
        for k, (src, dst) in enumerate(moves)
    ]
    acopies = row_copies(cown, cslot_a, asend, arecv, [(d, 0) for d in range(1, lat_n)])
    for copy in hcopies + acopies:
        copy.start()

    for copy in acopies:
        copy.wait_recv()
    total = cown[...]
    for d in range(1, lat_n):
        total = total + cslot_a[d - 1]
    crow[...] = total
    bcopies = row_copies(crow, cslot_b, bsend, brecv, [(0, d) for d in range(1, lon_n)])
    for copy in bcopies:
        copy.start()

    def ring_rows(buf, r):
        order = list(range(8, 8 + units + 1)) + [7]
        return lane_rows([buf[r, s : s + 1, :] for s in order])

    def smooth(field):
        pair = field + pltpu.roll(field, 1, 0)
        down = field + pltpu.roll(pair, 1, 0) + pltpu.roll(pair, ext_rows - 2, 0)
        pair = down + pltpu.roll(down, 1, 1)
        both = down + pltpu.roll(pair, 1, 1) + pltpu.roll(pair, ext_cols - 2, 1)
        return both * jnp.float32(1.0 / 25.0)

    for copy in hcopies:
        copy.wait_recv()
    lane_x = lax.broadcasted_iota(jnp.int32, (ext_rows, 128), 1)
    row_x = lax.broadcasted_iota(jnp.int32, (ext_rows, ext_cols), 0)
    low = lane < 64
    far_w, far_e, near_w, near_e, mid_w, mid_e = (sides[k] for k in range(6))
    wrap_w = [jnp.where(low, near_e, near_w)]
    wrap_i = [turn(jnp.where(low, near_w, near_e), 64)]
    for i in range(rows // 8):
        wrap_w.append(jnp.where(low, turn(mid_e, -8 * i), turn(mid_w, 120 - 8 * i)))
        wrap_i.append(jnp.where(low, turn(mid_e, 64 - 8 * i), turn(mid_w, 56 - 8 * i)))
    wrap_w = jnp.concatenate(wrap_w + [jnp.where(low, far_e, far_w)], axis=0)
    wrap_i = jnp.concatenate(wrap_i + [turn(jnp.where(low, far_w, far_e), 64)], axis=0)
    keep_e = (lane_x < M) & (lon < lon_n - 1)
    keep_w = (lane_x >= 128 - M) & (lon > 0)
    wrap = jnp.where(keep_e | keep_w, wrap_i, -1.0)
    whole = jnp.concatenate([halo[1, :, 0:cols], wrap], axis=1)
    gone = ((row_x < M) & (lat == 0)) | ((row_x >= M + rows) & (lat == lat_n - 1))
    whole = jnp.where(gone, -1.0, whole)
    band = 2 * M

    def classed(which, picked, base, other):
        even, odd = picked
        return jnp.where(which == even, base, jnp.where(which == odd, base + 1, other))

    def home_rows(at):
        mids = []
        for j in range(units):
            c = j * BLK + BLK // 2
            mids.append(halo[1, at : at + 1, c // 128 * 128 : c // 128 * 128 + 128])
            mids[j] = mids[j][:, c % 128 : c % 128 + 1]
        return lane_rows(mids + [wrap_i[at : at + 1, 4:5], wrap_i[at : at + 1, 123:124]])

    kinds = classed(whole, home_rows(M + BLK // 2), 0, -1)
    code[...] = kinds
    code[0:band] = classed(whole[0:band], home_rows(M // 2 - 1), 2, kinds[0:band])
    code[ext_rows - band :] = classed(
        whole[ext_rows - band :], home_rows(M + rows + M // 2), 4, kinds[ext_rows - band :]
    )
    for p in range(2):
        reach[p] = smooth(jnp.where(code[...] == p, 1.0, 0.0))

    def fold(x):
        return jnp.sum(x.reshape(x.shape[0] // 8, 8, ext_cols), axis=0)

    def census(field, k):
        kind = code[...]
        both = []
        for p in range(2):
            near = field * reach[p]
            head, tail = near[0:band], near[ext_rows - band :]
            hkind, tkind = kind[0:band], kind[ext_rows - band :]
            parts = [fold(jnp.where(kind == p, field, 0.0))]
            for v in (p, 1 - p):
                parts.append(fold(jnp.where(hkind == 2 + v, head, 0.0)))
                parts.append(fold(jnp.where(kind == v, near, 0.0)))
                parts.append(fold(jnp.where(tkind == 4 + v, tail, 0.0)))
            both.append(parts)
        sums = []
        for q in range(7):
            even, odd = (
                [both[p][q][:, 128 * t : 128 * t + 128] for t in range(tiles + 1)] for p in range(2)
            )
            level = []
            for t in range(tiles):
                level.append(jnp.where(lane < 96, even[t], even[t - 1]))
                level.append(jnp.where(lane < 32, odd[t + 1], odd[t]))
            step = len(level) // 2
            while step:
                bit = (sub & step) == 0
                joined = []
                for i in range(step):
                    a, b = level[i], level[i + step]
                    give = jnp.where(bit, b, a)
                    up = pltpu.roll(give, 8 - step, 0)
                    if step < 4:
                        up = jnp.where(bit, up, pltpu.roll(give, step, 0))
                    joined.append(jnp.where(bit, a, b) + up)
                level = joined
                step //= 2
            sums.append(level[0])
        inner = (lane >= 32) & (lane < 96)
        left = inner == ((sub & 1) == 1)
        links = jnp.broadcast_to(jnp.sum(sums[0], axis=1, keepdims=True), (8, 128))
        for d in range(3):
            cross = sums[4 + d]
            for b, x in enumerate(
                (jnp.where(left, cross, 0.0), sums[1 + d], jnp.where(left, 0.0, cross))
            ):
                links = jnp.where(lane == 3 * d + b, jnp.sum(x, axis=1, keepdims=True), links)
        ebuf[k, 2, 8:16, :] = links
        copies = far_copies(ebuf.at[k], esend.at[k], erecv.at[k])
        for copy in copies:
            copy.start()
        return copies

    lane_u = lax.broadcasted_iota(jnp.int32, (24, 128), 1)

    def solve(k):
        mail = [ebuf[k, r] for r in range(5)]
        first = [cbuf[r] / jnp.where(lane_u < 64, turn(mail[r], 64), mail[r]) for r in range(5)]
        for r in range(1, 4):
            fbuf[2 * k, r - 1] = first[r]
            mix = jnp.zeros((24, 128), jnp.float32)
            for a in range(3):
                for b in range(3):
                    f = first[r + a - 1]
                    f = f if b == 1 else pltpu.roll(f, 1 if b == 0 else 23, 0)
                    mix = jnp.where(lane_u == 3 * a + b, f, mix)
            second = jnp.sum(mix * mail[r], axis=1, keepdims=True)
            fbuf[2 * k + 1, r - 1] = cbuf[r] / second

    def scaled(field, i):
        kind = code[...]
        rows_f = [ring_rows(fbuf.at[i], r) for r in range(3)]

        def chosen(which, base, picked, other):
            return jnp.where(
                which == base, picked[0], jnp.where(which == base + 1, picked[1], other)
            )

        fac = chosen(kind, 0, rows_f[1], 0.0)
        head = chosen(kind[0:band], 2, rows_f[0], fac[0:band])
        tail = chosen(kind[ext_rows - band :], 4, rows_f[2], fac[ext_rows - band :])
        fac = jnp.concatenate([head, fac[band : ext_rows - band], tail], axis=0)
        return field * fac

    sbuf[...] = jnp.concatenate([halo[0, :, 0:cols], wrap_w], axis=1)
    pending = census(sbuf[...], 0)

    for copy in bcopies:
        copy.wait_recv()
    table = crow[0]
    for d in range(1, lon_n):
        table = table + cslot_b[d - 1, 0]
    uid = jnp.where(lane < units * lon_n, sub * (units * lon_n) + lane, -1).astype(jnp.float32)
    columns = (cslot_b[0, 1], crow[1], cslot_b[lon_n - 2, 1])
    for i in range(5):
        at = lax.rem(lat + (i - 2 + lat_n), lat_n)
        for b in range(3):
            homes[i, 8 * b : 8 * b + 8, :] = jnp.broadcast_to(
                jnp.sum(jnp.where(lane == at, columns[b], 0.0), axis=1, keepdims=True), (8, 128)
            )

    def look(r, carry):
        found = [jnp.zeros((8, 128), jnp.float32)] * 3
        for s in range(6, 10 + units):
            hit = jnp.where(uid == homes[r, s : s + 1, :], table, 0.0)
            hit = jnp.sum(hit, axis=0, keepdims=True)
            found[s // 8] = jnp.where(sub == s % 8, hit, found[s // 8])
        for i in range(3):
            cbuf[r, 8 * i : 8 * i + 8, :] = jnp.broadcast_to(
                jnp.sum(found[i], axis=1, keepdims=True), (8, 128)
            )
        return carry

    lax.fori_loop(0, 5, look, 0)

    for k in range((ROUNDS + 1) // 2):
        if k > 0:
            pending = census(sbuf[...], k)
        for copy in pending:
            copy.wait_recv()
        solve(k)
        field = smooth(scaled(sbuf[...], 2 * k))
        if 2 * k + 1 < ROUNDS:
            sbuf[...] = smooth(scaled(field, 2 * k + 1))
            sent = pending
        else:
            out_ref[...] = scaled(field, ROUNDS)[M : M + rows, 0:cols]

    for copy in hcopies + acopies + bcopies + sent + pending:
        copy.wait_send()


def shards(covariates, w_in, b_in, w_out, b_out, unit_ids, unit_counts):
    lat_n = lax.axis_size("lat")
    lon_n = lax.axis_size("lon")
    cov_n, rows, cols = covariates.shape
    hid = w_in.shape[1]
    ext_rows, ext_cols = rows + 2 * M, cols + 128
    kx = cov_n * GR + GR
    f32, i32, bf16 = jnp.float32, jnp.int32, jnp.bfloat16
    hbm = pl.BlockSpec(memory_space=pltpu.HBM)
    dma = pltpu.SemaphoreType.DMA
    pairs = (ROUNDS + 1) // 2
    far = len(FAR)
    return pl.pallas_call(
        functools.partial(kernel, lat_n, lon_n),
        out_shape=pltpu.VMEM((rows, cols), f32),
        in_specs=[hbm] * 8,
        out_specs=pl.BlockSpec(memory_space=pltpu.VMEM),
        scratch_shapes=[
            pltpu.VMEM((cov_n, rows, cols), bf16),
            pltpu.VMEM((cov_n, hid), bf16),
            pltpu.VMEM((1, hid), f32),
            pltpu.VMEM((1, hid), f32),
            pltpu.SMEM((hid,), f32),
            pltpu.VMEM((1, 1), f32),
            pltpu.SMEM((unit_counts.shape[0],), i32),
            pltpu.VMEM(((hid + LIN) * GR, kx), bf16),
            pltpu.VMEM((rows, cols), i32),
            pltpu.VMEM((2, ext_rows, ext_cols), f32),
            pltpu.VMEM((6, 8, 128), f32),
            pltpu.VMEM((6, 8, 128), f32),
            pltpu.VMEM((ext_rows, ext_cols), i32),
            pltpu.VMEM((ext_rows, ext_cols), f32),
            pltpu.VMEM((2, ext_rows, ext_cols), f32),
            pltpu.VMEM((5, 24, 128), f32),
            pltpu.VMEM((2, 8, 128), f32),
            pltpu.VMEM((2, 8, 128), f32),
            pltpu.VMEM((lat_n - 1, 2, 8, 128), f32),
            pltpu.VMEM((lon_n - 1, 2, 8, 128), f32),
            pltpu.VMEM((5, 24, 128), f32),
            pltpu.VMEM((pairs, 5, 24, 128), f32),
            pltpu.VMEM((2 * pairs, 3, 24, 128), f32),
            dma(()),
            dma((6,)),
            dma(()),
            dma((8,)),
            dma((8,)),
            dma((lat_n - 1,)),
            dma((lat_n - 1,)),
            dma((lon_n - 1,)),
            dma((lon_n - 1,)),
            dma((pairs, far)),
            dma((pairs, far)),
        ],
        compiler_params=pltpu.CompilerParams(
            collective_id=0, has_side_effects=True, vmem_limit_bytes=60 * 1024 * 1024
        ),
    )(covariates, w_in, b_in.reshape(1, hid), w_out.reshape(1, hid), w_out, b_out.reshape(1, 1), unit_ids, unit_counts)


def solution(mesh):
    return jax.shard_map(
        shards,
        mesh=mesh,
        in_specs=(P(None, "lat", "lon"), P(), P(), P(), P(), P("lat", "lon"), P(("lat", "lon"))),
        out_specs=P("lat", "lon"),
        check_vma=False,
    )
```
